32 devices in a mesh: req: 8 (over z, x), head: 4 (over y, core).
Axes of the slice: x: 2, y: 2, z: 4, core: 2. Of those that a mesh axis runs over, the one named last changes fastest.
Arguments:
- hidden: bfloat16 [56, 2048], P('req'), may hold values from -6 to 6
- queries: bfloat16 [56, 16, 576], P('req', 'head'), may hold values from -48 to 48
- latent_cache: bfloat16 [64, 128, 576], P(('req', 'head')), may hold values from -6 to 6
- page_table: int32 [56, 2], P('req'), may hold values from 0 to 7, as said below
- seq_lens: int32 [56], P('req'), may hold values from 2 to 256, as said below
- value_up: bfloat16 [16, 512, 128], P('head'), may hold values from -0.25 to 0.25
- out_proj: bfloat16 [2048, 2048], P('head'), may hold values from -0.125 to 0.125
- norm_gain: float32 [2048], replicated, may hold values from 0.25 to 1.75
- expert_ids: int32 [56, 6], P('req'), may hold values from 0 to 63, all different within a row; in each aligned block of 7 rows (0 to 6, 7 to 13, ...) at most 2 rows name the same one
- expert_mix: float32 [56, 6], P('req'), may hold values from 0.2 to 1
- gate_weight: bfloat16 [128, 2048, 704], P('req', None, 'head'), may hold values from -0.125 to 0.125
- up_weight: bfloat16 [128, 2048, 704], P('req', None, 'head'), may hold values from -0.125 to 0.125
- down_weight: bfloat16 [128, 704, 2048], P('req', 'head'), may hold values from -0.15625 to 0.15625
Outputs:
- layer_out: bfloat16 [56, 2048], P('req', 'head')
The draws below stay inside these ranges and needn't reach their ends.
Inputs may be any that keep to these rules, and one draw needn't show every extreme that they name: `page_table`: rows g * 7 to g * 7 + 6 form group g. The first ceil(seq_lens / 128) entries of a row are distinct pages, no page serves two requests of a group, and the remaining entries repeat the row's first page. `seq_lens`: the pages that the requests of one group need sum to at most 8. `expert_ids`: among the 7 rows of one device, at most 2 name the same expert.
All inputs are finite; a program needn't handle non-finite values.
Results may differ from the reference program's by a relative error of at most 0.02.
Values may be sent and summed in bfloat16 or wider, within the bound.
No kernel may reach another device: no remote copies, remote signals or barrier semaphores. Data moves between devices by JAX's collectives and lax.ppermute only.
A program may use at most 64 MiB of HBM per device.

```python
import math
import jax
import jax.numpy as jnp
import numpy as np
from jax import lax

D = 2048
HEADS = 16
RANK = 512
ROPE = 64
NOPE = 128
VHEAD = 128
EXPERTS = 64
FF = 1408
TOP = 6
PAGE = 128
CAP = 2
R_DEV = 7
KV = 576
REQS = 56
PAGES_GROUP = 8
MAXP = 2
PAGES_ALL = 64
N_REQ = 8


def page_layout(key):
    groups = REQS // R_DEV
    key_long, key_rest, key_perm = jax.random.split(jax.random.fold_in(key, 7), 3)
    long_at = jax.random.randint(key_long, (groups, 1), 0, R_DEV)
    positions = jnp.arange(R_DEV)[None, :]
    is_long = (positions == long_at).astype(jnp.int32)
    counts = 1 + (MAXP - 1) * is_long
    starts = jnp.cumsum(counts, axis=1) - counts
    perm_keys = jax.random.split(key_perm, groups)
    perms = jax.vmap(lambda single: jax.random.permutation(single, PAGES_GROUP))(perm_keys).astype(jnp.int32)
    offsets = jnp.arange(MAXP)[None, None, :]
    picks = starts[:, :, None] + jnp.minimum(offsets, counts[:, :, None] - 1)
    table = jnp.take_along_axis(perms, picks.reshape(groups, R_DEV * MAXP), axis=1).reshape(REQS, MAXP)
    remain = jax.random.randint(key_rest, (groups, R_DEV), 2, PAGE + 1)
    first_group = (jnp.arange(groups)[:, None] == 0).astype(jnp.int32) * is_long
    remain = remain + (PAGE - remain) * first_group
    lengths = ((counts - 1) * PAGE + remain).reshape(REQS)
    return (table.astype(jnp.int32), lengths.astype(jnp.int32))


def draw_page_table(key, part):
    return page_layout(key)[0]


def draw_seq_lens(key, part):
    return page_layout(key)[1]


def draw_latent_cache(key, part):
    key_base = jax.random.fold_in(jax.random.fold_in(key, 3), 0)
    filled = jnp.clip(jax.random.normal(key_base, (PAGES_ALL, PAGE, KV), jnp.float32), -6.0, 6.0)
    return filled.astype(jnp.bfloat16)


def draw_queries(key, part):
    key_drawn = jax.random.fold_in(jax.random.fold_in(key, 5), 0)
    filled = jnp.clip(jax.random.normal(key_drawn, (REQS, HEADS, KV), jnp.float32), -6.0, 6.0)
    return filled.astype(jnp.bfloat16)


def levels(own_key, shape, cuts, smallest, largest):
    def one(dim, parts):
        steps = jax.random.uniform(jax.random.fold_in(jax.random.fold_in(own_key, 6), dim), (parts,), jnp.float32, smallest / len(cuts), largest / len(cuts))
        return jnp.repeat(jnp.exp(steps), shape[dim] // parts).reshape((-1,) + (1,) * (len(shape) - dim - 1))

    level = one(*cuts[0])
    for cut in cuts[1:]:
        level = level * one(*cut)
    return level


def shared_out(own_key, own, number, rows, number_of, top, limit, lean):
    order = jax.random.permutation(own_key, number_of)
    heavy_load, ordinary = portions_of(number_of, rows * top, limit, lean, True), portions_of(number_of, rows * top, limit, lean, False)
    places = jnp.arange(number_of)

    def named(sizes, offset_by):
        used = int((sizes > 0).sum())
        fixed = max(1, used // 4)
        shifted = fixed + (places - fixed + offset_by * (used - fixed)) % max(1, number_of - fixed)
        return jnp.zeros((number_of,), jnp.int32).at[order[jnp.where(places < fixed, places, shifted)]].set(jnp.asarray(sizes, jnp.int32))

    sizes = jnp.where(number % 4 == 0, named(heavy_load, number // 4), named(ordinary, number - number // 4 - 1))
    mixed = jax.random.permutation(jax.random.fold_in(own, 3), number_of)
    donor, taker = mixed[0:number_of // 2 * 2:2], mixed[1:number_of // 2 * 2:2]
    slack = jnp.minimum(sizes[donor] - 1, limit - sizes[taker]) // 2
    slack = jnp.where((donor == order[0]) | (taker == order[0]) | (sizes[taker] == 0), 0, jnp.maximum(slack, 0))
    shifted = jax.random.randint(jax.random.fold_in(own, 4), (number_of // 2,), 0, 1 << 20) % (slack + 1)
    sizes = sizes.at[donor].add(-shifted).at[taker].add(shifted)
    labels = jnp.searchsorted(jnp.cumsum(sizes), jnp.arange(rows * top), side="right").astype(jnp.int32)
    grid = labels.reshape(top, rows).T
    grid = grid[jax.random.permutation(jax.random.fold_in(own, 1), rows)]
    offset_by = jax.random.randint(jax.random.fold_in(own, 2), (rows, 1), 0, top)
    return jnp.take_along_axis(grid, (jnp.arange(top)[None, :] + offset_by) % top, axis=1)


def portions_of(amount, total, most, slope, full):
    loads = [(1 << 20) // math.isqrt(grade ** slope) + 1 for grade in range(1, amount + 1)]
    largest = most if full else min(most, max(-(-total // amount), total * loads[0] // sum(loads)))
    least = 1 if total - largest >= amount - 1 else 0
    holding, rest = [largest] + [least] * (amount - 1), total - largest - least * (amount - 1)
    while rest > 0:
        free = [i for i in range(1, amount) if holding[i] < largest] or [i for i in range(1, amount) if holding[i] < most]
        mass, left = sum([loads[i] for i in free]), rest
        for i in free:
            more = min(most - holding[i], max(1, left * loads[i] // mass), rest)
            holding[i] = holding[i] + more
            rest = rest - more
    return np.array(holding)


def normal_values(stream_key, extent, scale, most, pieces=(), kind=jnp.bfloat16):
    values = jax.random.normal(stream_key, extent, jnp.float32) * scale
    if len(pieces) > 0:
        values = levels(stream_key, extent, pieces, -0.22, 0.18) * values
    return jnp.clip(values, min=-most, max=most).astype(kind)


def setup_inputs(seed: int = 0) -> dict:
    keys = jax.random.split(jax.random.key(seed), 14)
    hidden = normal_values(keys[0], (REQS, D), 1.0, 6.0, ((0, 8),))
    queries = draw_queries(jax.random.fold_in(keys[13], 71), 0)
    latent_cache = draw_latent_cache(jax.random.fold_in(keys[13], 71), 0)
    page_table = draw_page_table(jax.random.fold_in(keys[13], 71), 0)
    seq_lens = draw_seq_lens(jax.random.fold_in(keys[13], 71), 0)
    value_up = normal_values(keys[5], (HEADS, RANK, VHEAD), RANK ** -0.5, 0.25, ((0, 4),))
    out_proj = normal_values(keys[6], (HEADS * VHEAD, D), (HEADS * VHEAD) ** -0.5, 0.125, ((0, 4),))
    norm_gain = jnp.clip(1.0 + 0.15 * jax.random.normal(keys[7], (D,), jnp.float32), 0.25, 1.75)
    expert_ids_keys = jax.random.split(jax.random.fold_in(keys[8], 1), REQS // R_DEV)
    expert_ids_turns = jax.random.permutation(jax.random.fold_in(keys[8], 3), REQS // R_DEV)
    expert_ids = jax.vmap(lambda own, number: shared_out(jax.random.fold_in(keys[8], 2), own, number, R_DEV, EXPERTS, TOP, CAP, 2))(expert_ids_keys, expert_ids_turns).reshape((REQS, TOP))
    expert_mix = jnp.clip(0.2 + 0.8 * jax.random.uniform(keys[9], (REQS, TOP), jnp.float32) ** levels(keys[9], (REQS, TOP), ((0, 8),), -0.2, 0.2), 0.2, 1.0)
    gate_weight = normal_values(keys[10], (2 * EXPERTS, D, FF // 2), D ** -0.5, 0.125, ((0, 8), (2, 4)))
    up_weight = normal_values(keys[11], (2 * EXPERTS, D, FF // 2), D ** -0.5, 0.125, ((0, 8), (2, 4)))
    down_weight = normal_values(keys[12], (2 * EXPERTS, FF // 2, D), FF ** -0.5, 0.15625, ((0, 8), (1, 4)))
    return {"hidden": hidden, "queries": queries, "latent_cache": latent_cache, "page_table": page_table, "seq_lens": seq_lens, "value_up": value_up, "out_proj": out_proj, "norm_gain": norm_gain, "expert_ids": expert_ids, "expert_mix": expert_mix, "gate_weight": gate_weight, "up_weight": up_weight, "down_weight": down_weight}


norm_eps = 1e-06
masked_low = -1e+30

def one_group(packed):
    group_queries, group_table, group_lens, group_pool = packed
    gathered = group_pool[group_table].reshape(R_DEV, MAXP * PAGE, KV)
    scale = 1.0 / math.sqrt(NOPE + ROPE)
    scores = jnp.einsum('rhc,rtc->rht', group_queries.astype(jnp.float32), gathered.astype(jnp.float32), precision=lax.Precision.HIGHEST) * scale
    position = jnp.arange(MAXP * PAGE)
    valid = (position[None, :] < group_lens[:, None])[:, None, :]
    masked = jnp.where(valid, scores, masked_low)
    highest = lax.optimization_barrier(jnp.max(masked, axis=-1, keepdims=True))
    weights = jnp.where(valid, jnp.exp(masked - highest), 0.0)
    totals = lax.optimization_barrier(jnp.sum(weights, axis=-1))
    latent = gathered[:, :, :RANK].astype(jnp.float32)
    summed = jnp.einsum('rht,rtc->rhc', weights, latent, precision=lax.Precision.HIGHEST)
    return summed / totals[:, :, None]

def reference(hidden, queries, latent_cache, page_table, seq_lens, value_up, out_proj, norm_gain, expert_ids, expert_mix, gate_weight, up_weight, down_weight):
    groups = REQS // R_DEV
    packed = (queries.reshape(groups, R_DEV, HEADS, KV), page_table.reshape(groups, R_DEV, MAXP), seq_lens.reshape(groups, R_DEV), latent_cache.reshape(groups, PAGES_GROUP, PAGE, KV))
    attended = lax.map(one_group, packed).reshape(REQS, HEADS, RANK).astype(jnp.bfloat16)
    head_out = jnp.einsum('rhc,hcv->rhv', attended.astype(jnp.float32), value_up.astype(jnp.float32)).astype(jnp.bfloat16)
    head_out = head_out.reshape(REQS, HEADS * VHEAD)
    mixed = hidden.astype(jnp.float32) + jnp.dot(head_out, out_proj, preferred_element_type=jnp.float32)
    spread = lax.optimization_barrier(jnp.mean(mixed * mixed, axis=-1, keepdims=True))
    normed = (mixed * lax.rsqrt(spread + norm_eps) * norm_gain).astype(jnp.bfloat16)
    pair_count = REQS * TOP
    flat_experts = expert_ids.reshape(pair_count)
    flat_mix = expert_mix.reshape(pair_count)
    order = jnp.argsort(flat_experts, stable=True).astype(jnp.int32)
    counts = lax.optimization_barrier(jnp.sum((flat_experts[:, None] == jnp.arange(EXPERTS)[None, :]).astype(jnp.int32), axis=0)).astype(jnp.int32)
    starts = (jnp.cumsum(counts) - counts).astype(jnp.int32)
    room = N_REQ * CAP
    order_pad = jnp.concatenate([order, jnp.zeros((room,), jnp.int32)])

    def expert_step(running, expert):
        picked = lax.dynamic_slice(order_pad, (starts[expert],), (room,))
        live = jnp.arange(room) < counts[expert]
        tokens_of = picked // TOP
        source = normed[tokens_of]
        result = jnp.zeros((room, D), jnp.float32)
        for half_index in range(2):
            which = 2 * expert + half_index
            gate_part = jnp.dot(source, lax.dynamic_index_in_dim(gate_weight, which, 0, keepdims=False), preferred_element_type=jnp.float32)
            up_part = jnp.dot(source, lax.dynamic_index_in_dim(up_weight, which, 0, keepdims=False), preferred_element_type=jnp.float32)
            active = (jax.nn.silu(gate_part) * up_part).astype(jnp.bfloat16)
            half_out = jnp.dot(active, lax.dynamic_index_in_dim(down_weight, which, 0, keepdims=False), preferred_element_type=jnp.float32).astype(jnp.bfloat16)
            result = result + half_out.astype(jnp.float32)
        weight = jnp.where(live, flat_mix[picked], 0.0)
        running = running.at[tokens_of].add(result * weight[:, None])
        return (running, None)
    routed, unused = lax.scan(expert_step, jnp.zeros((REQS, D), jnp.float32), jnp.arange(EXPERTS).astype(jnp.int32))
    return (mixed + routed).astype(jnp.bfloat16)
```

```python
import functools
import math

import jax
import jax.numpy as jnp
from jax import lax
from jax.experimental import pallas as pl
from jax.experimental.pallas import tpu as pltpu
from jax.sharding import PartitionSpec as P

RANK = 512
ROPE = 64
NOPE = 128
VHEAD = 128
EXPERTS = 64
TOP = 6
PAGE = 128
LANES = 128
ROWS = 8

norm_eps = 1e-06
masked_low = -1e30

f32 = jnp.float32
bf16 = jnp.bfloat16
NT = (((1,), (1,)), ((), ()))
VMEM = pl.BlockSpec(memory_space=pltpu.VMEM)
SMEM = pl.BlockSpec(memory_space=pltpu.SMEM)
ANY = pl.BlockSpec(memory_space=pl.ANY)


def split3(value):
    high = value.astype(bf16).astype(f32)
    rest = value - high
    middle = rest.astype(bf16).astype(f32)
    return high, middle, (rest - middle).astype(bf16).astype(f32)


def attend_kernel(
    table,
    lens,
    ids,
    mix,
    q_own,
    q_far,
    cache_own,
    cache_near,
    own_out,
    own_lse,
    far_out,
    route_out,
    q_all,
    weighted,
    lse_all,
):
    head_at = lax.axis_index("head")
    requests, heads, width = q_own.shape
    pages_here = cache_own.shape[0]
    q_all[...] = jnp.zeros_like(q_all)
    for r in range(requests):
        q_all[r * ROWS : r * ROWS + heads, :] = q_own[r].astype(f32)
        q_all[r * ROWS + heads : r * ROWS + 2 * heads, :] = q_far[r].astype(f32)
    q_rows = q_all[...].astype(bf16)
    total_rows = q_all.shape[0]
    row_request = lax.broadcasted_iota(jnp.int32, (total_rows, PAGE), 0) // ROWS
    within = lax.broadcasted_iota(jnp.int32, (total_rows, PAGE), 1)
    scale = 1.0 / math.sqrt(NOPE + ROPE)
    keys, valids, scores = [], [], []
    for side, cache in ((0, cache_own), (1, cache_near)):
        holder = head_at if side == 0 else head_at ^ 1
        for p in range(pages_here):
            page = holder * pages_here + p
            owner = jnp.int32(-1)
            count = jnp.int32(0)
            for r in range(requests):
                for m in range(table.shape[1]):
                    left = lens[r] - m * PAGE
                    hit = jnp.logical_and(table[r, m] == page, left > 0)
                    owner = jnp.where(hit, r, owner)
                    count = jnp.where(hit, left, count)
            valid = (row_request == owner) & (within < count)
            keys.append(cache.at[p])
            valids.append(valid)
            score = jnp.dot(q_rows, cache[p], preferred_element_type=f32) * scale
            scores.append(jnp.where(valid, score, masked_low))
    highest = functools.reduce(jnp.maximum, scores).max(axis=-1, keepdims=True)
    total = jnp.zeros((total_rows, 1), f32)
    summed = jnp.zeros((total_rows, RANK), f32)
    for key, valid, score in zip(keys, valids, scores):
        weight = jnp.where(valid, jnp.exp(score - highest), 0.0)
        total = total + jnp.sum(weight, axis=-1, keepdims=True)
        high = weight.astype(bf16)
        low = (weight - high.astype(f32)).astype(bf16)
        latent = key[:RANK, :]
        summed = summed + lax.dot_general(high, latent, NT, preferred_element_type=f32)
        summed = summed + lax.dot_general(low, latent, NT, preferred_element_type=f32)
    some = total > 0.0
    safe = jnp.where(some, total, 1.0)
    summed = summed * (1.0 / safe)
    for c in range(RANK // LANES):
        weighted[c] = summed[:, c * LANES : (c + 1) * LANES]
    lse = jnp.where(some, highest + jnp.log(safe), masked_low)
    lse_all[...] = jnp.broadcast_to(lse, lse_all.shape)
    lane = lax.broadcasted_iota(jnp.int32, (ROWS, 128), 1)
    for h in range(heads):
        own_lse[h] = lse_all[pl.ds(h, ROWS, stride=ROWS), :]
        for c in range(RANK // LANES):
            span = slice(c * LANES, (c + 1) * LANES)
            own_out[h, :, span] = weighted[c, pl.ds(h, ROWS, stride=ROWS), :]
            far_out[h, :, span] = weighted[c, pl.ds(heads + h, ROWS, stride=ROWS), :].astype(bf16)
        high, middle, low = split3(lse_all[pl.ds(heads + h, ROWS, stride=ROWS), :])
        far_out[h, :, RANK:] = jnp.where(
            lane == 0, high, jnp.where(lane == 1, middle, jnp.where(lane == 2, low, 0.0))
        ).astype(bf16)
    lanes = lax.broadcasted_iota(jnp.int32, route_out.shape, 1)
    row = jnp.zeros(route_out.shape, f32)
    for r in range(requests):
        for i in range(TOP):
            row = jnp.where(lanes == r * EXPERTS + ids[r, i], mix[r, i], row)
    high, middle, low = split3(row)
    route_out[...] = jnp.where(
        head_at == 0, high, jnp.where(head_at == 1, middle, jnp.where(head_at == 2, low, 0.0))
    )


def project_kernel(own, own_lse, far, value_up, out_proj, mine, near, far_y, far_both, whole):
    heads = own.shape[0]
    head_at = lax.axis_index("head")
    parts = []
    for h in range(heads):
        stats = far[h, :, RANK:].astype(f32)
        lse_far = stats[:, 0:1] + stats[:, 1:2] + stats[:, 2:3]
        lse_own = own_lse[h][:, 0:1]
        highest = jnp.maximum(lse_own, lse_far)
        weight_own = jnp.exp(lse_own - highest)
        weight_far = jnp.exp(lse_far - highest)
        merged = weight_own * own[h] + weight_far * far[h, :, :RANK].astype(f32)
        attended = (merged * (1.0 / (weight_own + weight_far))).astype(bf16)
        parts.append(jnp.dot(attended, value_up[h], preferred_element_type=f32))
    head_out = jnp.concatenate(parts, axis=1).astype(bf16)
    whole[...] = jnp.dot(head_out, out_proj[...], preferred_element_type=f32)
    quarter = mine.shape[1]
    mine[...] = whole[:, pl.ds(pl.multiple_of(head_at * quarter, quarter), quarter)]
    for out, flip in ((near, 1), (far_y, 2), (far_both, 3)):
        start = pl.multiple_of((head_at ^ flip) * quarter, quarter)
        out[...] = whole[:, pl.ds(start, quarter)].astype(bf16)


def mix_kernel(mine, near, far_y, far_both, hidden, route, mixed_out, spread_out):
    head_at = lax.axis_index("head")
    requests = hidden.shape[0]
    quarter = mine.shape[1]
    start = pl.multiple_of(head_at * quarter, quarter)
    attn = mine[...] + near[...].astype(f32) + far_y[...].astype(f32) + far_both[...].astype(f32)
    residual = hidden[:, pl.ds(start, quarter)].astype(f32)
    mixed_out[...] = attn[:requests] + residual
    row = lax.broadcasted_iota(jnp.int32, (ROWS, quarter), 0)
    padded = jnp.concatenate(
        [residual, jnp.zeros((ROWS - requests, quarter), f32)], axis=0
    )
    block = jnp.where(row < requests, attn + padded, route[...]).astype(bf16)
    for n in range(spread_out.shape[0]):
        spread_out[n] = block


def expert_kernel(
    chunk,
    tokens,
    gain,
    gate,
    up,
    down,
    out,
    rows_all,
    mix_all,
    total,
    gate_buf,
    up_buf,
    down_buf,
    sems,
):
    req_count = lax.axis_size("req")
    head_count = lax.axis_size("head")
    req_at = lax.axis_index("req")
    slots, depth, model = gate.shape
    quarter = tokens.shape[2]
    requests = ROWS - 1
    live = requests * req_count
    units = slots * depth
    steps = units // chunk
    flat = [w.reshape(units, model) for w in (gate, up, down)]

    def copies(step):
        slot = step % 2
        return [
            pltpu.make_async_copy(
                w.at[pl.ds(step * chunk, chunk), :], buf.at[slot], sems.at[n, slot]
            )
            for n, (w, buf) in enumerate(zip(flat, (gate_buf, up_buf, down_buf)))
        ]

    for copy in copies(0):
        copy.start()
    for i in range(req_count):
        for j in range(head_count):
            block = tokens[i * head_count + j].astype(f32)
            for c in range(quarter // LANES):
                rows_all[j * quarter // LANES + c, pl.ds(i, ROWS, stride=req_count), :] = block[
                    :, c * LANES : (c + 1) * LANES
                ]
    for r in range(requests):
        for k in range(3):
            start = k * quarter + r * EXPERTS
            lane = start % LANES
            mix_all[r * req_count : (r + 1) * req_count, k * EXPERTS : (k + 1) * EXPERTS] = rows_all[
                start // LANES, live : live + req_count, lane : lane + EXPERTS
            ]
    mixed = jnp.concatenate([rows_all[c, :live, :] for c in range(model // LANES)], axis=1)
    spread = jnp.mean(mixed * mixed, axis=-1, keepdims=True)
    normed = (mixed * lax.rsqrt(spread + norm_eps) * gain[...]).astype(bf16)
    mix_rows = mix_all[...].astype(bf16)
    for step in range(steps):
        slot = step % 2
        if step + 1 < steps:
            for copy in copies(step + 1):
                copy.start()
        for copy in copies(step):
            copy.wait()
        unit = step * chunk + lax.broadcasted_iota(jnp.int32, (3 * EXPERTS, chunk), 1)
        expert = lax.broadcasted_iota(jnp.int32, (3 * EXPERTS, chunk), 0) % EXPERTS
        here = expert == (req_at * slots + unit // depth) // 2
        weight = jnp.dot(
            mix_rows, jnp.where(here, 1.0, 0.0).astype(bf16), preferred_element_type=f32
        )
        gate_part = lax.dot_general(normed, gate_buf[slot], NT, preferred_element_type=f32)
        up_part = lax.dot_general(normed, up_buf[slot], NT, preferred_element_type=f32)
        active = gate_part / (1.0 + jnp.exp(-gate_part)) * up_part * weight
        product = jnp.dot(active.astype(bf16), down_buf[slot], preferred_element_type=f32)
        for c in range(model // LANES):
            share = product[:, c * LANES : (c + 1) * LANES]
            total[c, :live, :] = share if step == 0 else total[c, :live, :] + share
    for c in range(model // LANES):
        total[c, live:, :] = jnp.zeros((req_count, LANES), f32)
    for i in range(req_count):
        for j in range(head_count):
            for c in range(quarter // LANES):
                out[i * head_count + j, :, c * LANES : (c + 1) * LANES] = total[
                    j * quarter // LANES + c, pl.ds(i, ROWS, stride=req_count), :
                ].astype(bf16)


def final_kernel(parts, mixed, out):
    total = jnp.sum(parts[...].astype(f32), axis=0)
    out[...] = (mixed[...] + total[: mixed.shape[0]]).astype(bf16)


def limit(mebibytes):
    return pltpu.CompilerParams(vmem_limit_bytes=mebibytes * 2**20)


def per_device(
    hidden,
    queries,
    latent_cache,
    page_table,
    seq_lens,
    value_up,
    out_proj,
    norm_gain,
    expert_ids,
    expert_mix,
    gate_weight,
    up_weight,
    down_weight,
):
    head_count = lax.axis_size("head")
    req_count = lax.axis_size("req")
    both = ("req", "head")
    requests, heads, width = queries.shape
    model = hidden.shape[1]
    quarter = model // head_count
    devices = req_count * head_count
    assert head_count == 4 and requests == ROWS - 1 and requests * EXPERTS <= quarter

    def swap(value, flip):
        return lax.ppermute(value, "head", [(n, n ^ flip) for n in range(head_count)])

    cache = jnp.swapaxes(latent_cache, 1, 2)
    q_far = swap(queries, 2)
    cache_near = swap(cache, 1)
    rows = ROWS * ROWS
    own, own_lse, far, route = pl.pallas_call(
        attend_kernel,
        out_shape=(
            jax.ShapeDtypeStruct((heads, ROWS, RANK), f32),
            jax.ShapeDtypeStruct((heads, ROWS, 128), f32),
            jax.ShapeDtypeStruct((heads, ROWS, RANK + 128), bf16),
            jax.ShapeDtypeStruct((1, quarter), f32),
        ),
        in_specs=[SMEM] * 4 + [VMEM] * 4,
        out_specs=[VMEM] * 4,
        scratch_shapes=[
            pltpu.VMEM((rows, width), f32),
            pltpu.VMEM((RANK // LANES, rows, LANES), f32),
            pltpu.VMEM((rows, LANES), f32),
        ],
        compiler_params=limit(8),
        name="attend",
    )(page_table, seq_lens, expert_ids, expert_mix, queries, q_far, cache, cache_near)
    far = swap(far, 2)
    piece = jax.ShapeDtypeStruct((ROWS, quarter), bf16)
    mine, near, far_y, far_both = pl.pallas_call(
        project_kernel,
        out_shape=(jax.ShapeDtypeStruct((ROWS, quarter), f32), piece, piece, piece),
        in_specs=[VMEM] * 5,
        out_specs=[VMEM] * 4,
        scratch_shapes=[pltpu.VMEM((ROWS, model), f32)],
        compiler_params=limit(8),
        name="project",
    )(own, own_lse, far, value_up, out_proj)
    near, far_y, far_both = swap(near, 1), swap(far_y, 2), swap(far_both, 3)
    mixed, spread = pl.pallas_call(
        mix_kernel,
        out_shape=(
            jax.ShapeDtypeStruct((requests, quarter), f32),
            jax.ShapeDtypeStruct((devices, ROWS, quarter), bf16),
        ),
        in_specs=[VMEM] * 6,
        out_specs=[VMEM] * 2,
        compiler_params=limit(12),
        name="mix",
    )(mine, near, far_y, far_both, hidden, route)
    tokens = lax.all_to_all(spread, both, split_axis=0, concat_axis=0, tiled=True)
    slots, _, depth = gate_weight.shape
    chunk = 256 if (slots * depth) % 256 == 0 else depth
    parts = pl.pallas_call(
        functools.partial(expert_kernel, chunk),
        out_shape=jax.ShapeDtypeStruct((devices, ROWS, quarter), bf16),
        in_specs=[VMEM, VMEM, ANY, ANY, ANY],
        out_specs=VMEM,
        scratch_shapes=[
            pltpu.VMEM((model // LANES, ROWS * req_count, LANES), f32),
            pltpu.VMEM((requests * req_count, 3 * EXPERTS), f32),
            pltpu.VMEM((model // LANES, ROWS * req_count, LANES), f32),
            pltpu.VMEM((2, chunk, model), bf16),
            pltpu.VMEM((2, chunk, model), bf16),
            pltpu.VMEM((2, chunk, model), bf16),
            pltpu.SemaphoreType.DMA((3, 2)),
        ],
        compiler_params=limit(50),
        name="experts",
    )(
        tokens,
        norm_gain.reshape(1, model),
        jnp.swapaxes(gate_weight, 1, 2),
        jnp.swapaxes(up_weight, 1, 2),
        down_weight,
    )
    parts = lax.all_to_all(parts, both, split_axis=0, concat_axis=0, tiled=True)
    return pl.pallas_call(
        final_kernel,
        out_shape=jax.ShapeDtypeStruct((requests, quarter), bf16),
        in_specs=[VMEM] * 2,
        out_specs=VMEM,
        compiler_params=limit(24),
        name="final",
    )(parts, mixed)


def solution(mesh):
    return jax.shard_map(
        per_device,
        mesh=mesh,
        in_specs=(
            P("req", None),
            P("req", "head", None),
            P(("req", "head"), None, None),
            P("req", None),
            P("req"),
            P("head", None, None),
            P("head", None),
            P(),
            P("req", None),
            P("req", None),
            P("req", None, "head"),
            P("req", None, "head"),
            P("req", "head", None),
        ),
        out_specs=P("req", "head"),
        check_vma=False,
    )
```

```python
import functools
import math

import jax
import jax.numpy as jnp
from jax import lax
from jax.experimental import pallas as pl
from jax.experimental.pallas import tpu as pltpu
from jax.sharding import PartitionSpec as P

RANK = 512
ROPE = 64
NOPE = 128
VHEAD = 128
EXPERTS = 64
TOP = 6
PAGE = 128
LANES = 128
ROWS = 8

norm_eps = 1e-06
masked_low = -1e30

f32 = jnp.float32
bf16 = jnp.bfloat16
NT = (((1,), (1,)), ((), ()))
VMEM = pl.BlockSpec(memory_space=pltpu.VMEM)
SMEM = pl.BlockSpec(memory_space=pltpu.SMEM)
ANY = pl.BlockSpec(memory_space=pl.ANY)


def split3(value):
    high = value.astype(bf16).astype(f32)
    rest = value - high
    middle = rest.astype(bf16).astype(f32)
    return high, middle, (rest - middle).astype(bf16).astype(f32)


def start_all(pairs, sems):
    copies = [
        pltpu.make_async_copy(src, dst, sems.at[n]) for n, (src, dst) in enumerate(pairs)
    ]
    for copy in copies:
        copy.start()
    return copies


def stage_kernel(*refs):
    table_in, lens_in, ids_in, mix_in = refs[:4]
    bias_out, route_out = refs[10:12]
    table, lens, ids, mix, small_sems, sems = refs[18:]
    small = start_all(
        ((table_in, table), (lens_in, lens), (ids_in, ids), (mix_in, mix)), small_sems
    )
    large = start_all(tuple(zip(refs[4:10], refs[12:18])), sems)
    for copy in small:
        copy.wait()
    head_at = lax.axis_index("head")
    width, requests = table.shape
    pages_here = bias_out.shape[0] // 2
    row_request = lax.broadcasted_iota(jnp.int32, bias_out.shape[1:], 0) // ROWS
    within = lax.broadcasted_iota(jnp.int32, bias_out.shape[1:], 1)
    for side in range(2):
        for p in range(pages_here):
            page = (head_at ^ side) * pages_here + p
            owner = jnp.int32(-1)
            count = jnp.int32(0)
            for r in range(requests):
                for m in range(width):
                    left = lens[r] - m * PAGE
                    hit = jnp.logical_and(table[m, r] == page, left > 0)
                    owner = jnp.where(hit, r, owner)
                    count = jnp.where(hit, left, count)
            valid = (row_request == owner) & (within < count)
            bias_out[side * pages_here + p] = jnp.where(valid, 1.0, 0.0)
    lanes = lax.broadcasted_iota(jnp.int32, route_out.shape, 1)
    row = jnp.zeros(route_out.shape, f32)
    for r in range(requests):
        for i in range(TOP):
            row = jnp.where(lanes == r * EXPERTS + ids[r, i], mix[r, i], row)
    high, middle, low = split3(row)
    route_out[...] = jnp.where(
        head_at == 0, high, jnp.where(head_at == 1, middle, jnp.where(head_at == 2, low, 0.0))
    )
    for copy in large:
        copy.wait()


def fetch_kernel(spans, *refs):
    count = len(spans)
    sources, outs, sems = refs[:count], refs[count + 1 : 2 * count + 1], refs[2 * count + 1]
    pairs = []
    for source, out, (first, last) in zip(sources, outs, spans):
        flat = source.reshape(source.shape[0] * source.shape[1], source.shape[2])
        pairs.append((flat.at[pl.ds(first, last - first), :], out))
    for copy in start_all(tuple(pairs), sems):
        copy.wait()


def attend_kernel(
    usable,
    q_own,
    q_far,
    cache_own,
    cache_near,
    own_out,
    own_lse,
    far_out,
    q_all,
    weighted,
    lse_all,
):
    requests, heads, width = q_own.shape
    pages_here = cache_own.shape[0]
    q_all[requests * ROWS :, :] = jnp.zeros((ROWS * (ROWS - requests), width), f32)
    for r in range(requests):
        q_all[r * ROWS : r * ROWS + heads, :] = q_own[r].astype(f32)
        q_all[r * ROWS + heads : r * ROWS + 2 * heads, :] = q_far[r].astype(f32)
    q_rows = q_all[...].astype(bf16)
    total_rows = q_all.shape[0]
    scale = 1.0 / math.sqrt(NOPE + ROPE)
    keys = [cache.at[p] for cache in (cache_own, cache_near) for p in range(pages_here)]
    valids = [usable[n] > 0.0 for n in range(2 * pages_here)]
    scores = []
    for key, valid in zip(keys, valids):
        score = jnp.dot(q_rows, key[...], preferred_element_type=f32) * scale
        scores.append(jnp.where(valid, score, masked_low))
    highest = functools.reduce(jnp.maximum, scores).max(axis=-1, keepdims=True)
    total = jnp.zeros((total_rows, 1), f32)
    summed = jnp.zeros((total_rows, RANK), f32)
    for key, valid, score in zip(keys, valids, scores):
        weight = jnp.where(valid, jnp.exp(score - highest), 0.0)
        total = total + jnp.sum(weight, axis=-1, keepdims=True)
        high = weight.astype(bf16)
        low = (weight - high.astype(f32)).astype(bf16)
        latent = key[:RANK, :]
        summed = summed + lax.dot_general(high, latent, NT, preferred_element_type=f32)
        summed = summed + lax.dot_general(low, latent, NT, preferred_element_type=f32)
    some = total > 0.0
    safe = jnp.where(some, total, 1.0)
    summed = summed * (1.0 / safe)
    for c in range(RANK // LANES):
        weighted[c] = summed[:, c * LANES : (c + 1) * LANES]
    lse = jnp.where(some, highest + jnp.log(safe), masked_low)
    lse_all[...] = jnp.broadcast_to(lse, lse_all.shape)
    lane = lax.broadcasted_iota(jnp.int32, (ROWS, LANES), 1)
    for h in range(heads):
        own_lse[h] = lse_all[pl.ds(h, ROWS, stride=ROWS), :]
        for c in range(RANK // LANES):
            span = slice(c * LANES, (c + 1) * LANES)
            own_out[h, :, span] = weighted[c, pl.ds(h, ROWS, stride=ROWS), :]
            far_out[h, :, span] = weighted[c, pl.ds(heads + h, ROWS, stride=ROWS), :].astype(bf16)
        high, middle, low = split3(lse_all[pl.ds(heads + h, ROWS, stride=ROWS), :])
        far_out[h, :, RANK:] = jnp.where(
            lane == 0, high, jnp.where(lane == 1, middle, jnp.where(lane == 2, low, 0.0))
        ).astype(bf16)


def project_kernel(own, own_lse, far, value_up, out_proj, _, mine, near, far_y, far_both, whole):
    heads = own.shape[0]
    head_at = lax.axis_index("head")
    parts = []
    for h in range(heads):
        stats = far[h, :, RANK:].astype(f32)
        lse_far = stats[:, 0:1] + stats[:, 1:2] + stats[:, 2:3]
        lse_own = own_lse[h][:, 0:1]
        highest = jnp.maximum(lse_own, lse_far)
        weight_own = jnp.exp(lse_own - highest)
        weight_far = jnp.exp(lse_far - highest)
        merged = weight_own * own[h] + weight_far * far[h, :, :RANK].astype(f32)
        attended = (merged * (1.0 / (weight_own + weight_far))).astype(bf16)
        parts.append(jnp.dot(attended, value_up[h], preferred_element_type=f32))
    head_out = jnp.concatenate(parts, axis=1).astype(bf16)
    whole[...] = jnp.dot(head_out, out_proj[...], preferred_element_type=f32)
    quarter = mine.shape[1]
    mine[...] = whole[:, pl.ds(pl.multiple_of(head_at * quarter, quarter), quarter)]
    for out, flip in ((near, 1), (far_y, 2), (far_both, 3)):
        start = pl.multiple_of((head_at ^ flip) * quarter, quarter)
        out[...] = whole[:, pl.ds(start, quarter)].astype(bf16)


def mix_kernel(mine, near, far_y, far_both, hidden, route, _, mixed_out, spread_out):
    head_at = lax.axis_index("head")
    requests = hidden.shape[0]
    quarter = mine.shape[1]
    start = pl.multiple_of(head_at * quarter, quarter)
    attn = mine[...] + near[...].astype(f32) + far_y[...].astype(f32) + far_both[...].astype(f32)
    residual = hidden[:, pl.ds(start, quarter)].astype(f32)
    mixed_out[...] = attn[:requests] + residual
    row = lax.broadcasted_iota(jnp.int32, (ROWS, quarter), 0)
    padded = jnp.concatenate(
        [residual, jnp.zeros((ROWS - requests, quarter), f32)], axis=0
    )
    block = jnp.where(row < requests, attn + padded, route[...]).astype(bf16)
    for n in range(spread_out.shape[0]):
        spread_out[n] = block


def expert_kernel(
    chunk,
    tokens,
    gain,
    gate_a,
    up_a,
    gate_b,
    up_b,
    gate,
    up,
    down,
    out,
    rows_all,
    mix_all,
    active_all,
    total,
    gate_c,
    up_c,
    down_all,
    sems,
):
    req_count = lax.axis_size("req")
    head_count = lax.axis_size("head")
    req_at = lax.axis_index("req")
    slots, depth, model = down.shape
    quarter = tokens.shape[2]
    requests = ROWS - 1
    live = requests * req_count
    units = slots * depth
    ready = gate_a.shape[0] + gate_b.shape[0]
    pairs = []
    for first in range(ready, units, chunk):
        for source, buffer in ((gate, gate_c), (up, up_c)):
            flat = source.reshape(units, model)
            pairs.append((flat.at[pl.ds(first, chunk), :], buffer.at[pl.ds(first - ready, chunk), :]))
    chunks = units // chunk
    edges = [chunks * n // 3 * chunk for n in range(4)]
    groups = list(zip(edges, edges[1:]))
    for first, last in groups:
        span = pl.ds(first, last - first)
        pairs.append((down.reshape(units, model).at[span, :], down_all.at[span, :]))
    loads = start_all(tuple(pairs), sems)
    for i in range(req_count):
        for j in range(head_count):
            block = tokens[i * head_count + j].astype(f32)
            for c in range(quarter // LANES):
                rows_all[j * quarter // LANES + c, pl.ds(i, ROWS, stride=req_count), :] = block[
                    :, c * LANES : (c + 1) * LANES
                ]
    for r in range(requests):
        for k in range(3):
            start = k * quarter + r * EXPERTS
            lane = start % LANES
            mix_all[r * req_count : (r + 1) * req_count, k * EXPERTS : (k + 1) * EXPERTS] = rows_all[
                start // LANES, live : live + req_count, lane : lane + EXPERTS
            ]
    mixed = jnp.concatenate([rows_all[c, :live, :] for c in range(model // LANES)], axis=1)
    spread = jnp.mean(mixed * mixed, axis=-1, keepdims=True)
    normed = (mixed * lax.rsqrt(spread + norm_eps) * gain[...]).astype(bf16)
    mix_rows = mix_all[...].astype(bf16)
    split = gate_a.shape[0]
    for first in range(0, units, chunk):
        if first < split:
            gate_at, up_at, offset = gate_a, up_a, first
        elif first < ready:
            gate_at, up_at, offset = gate_b, up_b, first - split
        else:
            gate_at, up_at, offset = gate_c, up_c, first - ready
            for _ in range(2):
                loads.pop(0).wait()
        unit = first + lax.broadcasted_iota(jnp.int32, (chunk, 3 * EXPERTS), 0)
        expert = lax.broadcasted_iota(jnp.int32, (chunk, 3 * EXPERTS), 1) % EXPERTS
        here = jnp.where(expert == (req_at * slots + unit // depth) // 2, 1.0, 0.0).astype(bf16)
        weight = lax.dot_general(here, mix_rows, NT, preferred_element_type=f32)
        gate_part = lax.dot_general(
            gate_at[offset : offset + chunk, :], normed, NT, preferred_element_type=f32
        )
        up_part = lax.dot_general(
            up_at[offset : offset + chunk, :], normed, NT, preferred_element_type=f32
        )
        active = gate_part / (1.0 + jnp.exp(-gate_part)) * up_part * weight
        active_all[:, first : first + chunk] = active.T.astype(bf16)
    for c in range(model // LANES):
        total[c, live:, :] = jnp.zeros((req_count, LANES), f32)
    for n, (first, last) in enumerate(groups):
        loads.pop(0).wait()
        product = jnp.dot(
            active_all[:, first:last], down_all[first:last, :], preferred_element_type=f32
        )
        for c in range(model // LANES):
            share = product[:, c * LANES : (c + 1) * LANES]
            total[c, :live, :] = share if n == 0 else total[c, :live, :] + share
    for i in range(req_count):
        for j in range(head_count):
            for c in range(quarter // LANES):
                out[i * head_count + j, :, c * LANES : (c + 1) * LANES] = total[
                    j * quarter // LANES + c, pl.ds(i, ROWS, stride=req_count), :
                ].astype(bf16)


def final_kernel(parts, mixed, out):
    total = jnp.sum(parts[...].astype(f32), axis=0)
    out[...] = (mixed[...] + total[: mixed.shape[0]]).astype(bf16)


def limit(mebibytes):
    return pltpu.CompilerParams(vmem_limit_bytes=mebibytes * 2**20)


def per_device(
    hidden,
    queries,
    latent_cache,
    page_table,
    seq_lens,
    value_up,
    out_proj,
    norm_gain,
    expert_ids,
    expert_mix,
    gate_weight,
    up_weight,
    down_weight,
):
    head_count = lax.axis_size("head")
    req_count = lax.axis_size("req")
    both = ("req", "head")
    requests, heads, width = queries.shape
    model = hidden.shape[1]
    quarter = model // head_count
    devices = req_count * head_count
    assert head_count == 4 and requests == ROWS - 1 and requests * EXPERTS <= quarter

    def swap(value, flip):
        return lax.ppermute(value, "head", [(n, n ^ flip) for n in range(head_count)])

    def on_hbm(*values):
        return [pltpu.with_memory_space_constraint(value, pltpu.HBM) for value in values]

    def fetch(after, *pieces):
        spans = tuple(span for _, span in pieces)
        shapes = tuple(pltpu.VMEM((last - first, model), bf16) for first, last in spans)
        size = sum(last - first for first, last in spans) * model * 2
        return pl.pallas_call(
            functools.partial(fetch_kernel, spans),
            out_shape=shapes,
            in_specs=[ANY] * (len(pieces) + 1),
            out_specs=[VMEM] * len(pieces),
            scratch_shapes=[pltpu.SemaphoreType.DMA((len(pieces),))],
            compiler_params=limit(4),
            cost_estimate=pl.CostEstimate(flops=0, bytes_accessed=size, transcendentals=0),
            name="fetch",
        )(*on_hbm(*(weight for weight, _ in pieces)), after)

    slots, _, depth = gate_weight.shape
    units = slots * depth
    chunk = units // 11
    split_a, split_b = 3 * chunk, 6 * chunk
    gate = jnp.swapaxes(gate_weight, 1, 2)
    up = jnp.swapaxes(up_weight, 1, 2)
    cache = jnp.swapaxes(latent_cache, 1, 2)
    pages_here = cache.shape[0]
    rows = ROWS * ROWS
    q_far = swap(queries, 2)
    cache_near = swap(cache, 1)
    large = (queries, cache, value_up, out_proj, hidden, norm_gain.reshape(1, model))
    usable, route, q_own, cache_own, value_up, out_proj, hidden, gain = pl.pallas_call(
        stage_kernel,
        out_shape=(
            pltpu.VMEM((2 * pages_here, rows, PAGE), f32),
            pltpu.VMEM((1, quarter), f32),
            *(pltpu.VMEM(value.shape, value.dtype) for value in large),
        ),
        in_specs=[ANY] * 10,
        out_specs=[VMEM] * 8,
        scratch_shapes=[
            pltpu.SMEM(page_table.shape[::-1], jnp.int32),
            pltpu.SMEM(seq_lens.shape, jnp.int32),
            pltpu.SMEM(expert_ids.shape, jnp.int32),
            pltpu.SMEM(expert_mix.shape, f32),
            pltpu.SemaphoreType.DMA((4,)),
            pltpu.SemaphoreType.DMA((6,)),
        ],
        compiler_params=limit(4),
        cost_estimate=pl.CostEstimate(flops=0, bytes_accessed=3 * 2**20, transcendentals=0),
        name="stage",
    )(*on_hbm(page_table.T, seq_lens, expert_ids, expert_mix, *large))
    own, own_lse, far = pl.pallas_call(
        attend_kernel,
        out_shape=(
            jax.ShapeDtypeStruct((heads, ROWS, RANK), f32),
            jax.ShapeDtypeStruct((heads, ROWS, LANES), f32),
            jax.ShapeDtypeStruct((heads, ROWS, RANK + LANES), bf16),
        ),
        in_specs=[VMEM] * 5,
        out_specs=[VMEM] * 3,
        scratch_shapes=[
            pltpu.VMEM((rows, width), f32),
            pltpu.VMEM((RANK // LANES, rows, LANES), f32),
            pltpu.VMEM((rows, LANES), f32),
        ],
        compiler_params=limit(8),
        name="attend",
    )(usable, q_own, q_far, cache_own, cache_near)
    gate_a, up_a = fetch(far, (gate, (0, split_a)), (up, (0, split_a)))
    far = swap(far, 2)
    piece = jax.ShapeDtypeStruct((ROWS, quarter), bf16)
    mine, near, far_y, far_both = pl.pallas_call(
        project_kernel,
        out_shape=(jax.ShapeDtypeStruct((ROWS, quarter), f32), piece, piece, piece),
        in_specs=[VMEM] * 6,
        out_specs=[VMEM] * 4,
        scratch_shapes=[pltpu.VMEM((ROWS, model), f32)],
        compiler_params=limit(8),
        name="project",
    )(own, own_lse, far, value_up, out_proj, gate_a)
    gate_b, up_b = fetch(near, (gate, (split_a, split_b)), (up, (split_a, split_b)))
    near, far_y, far_both = swap(near, 1), swap(far_y, 2), swap(far_both, 3)
    mixed, spread = pl.pallas_call(
        mix_kernel,
        out_shape=(
            jax.ShapeDtypeStruct((requests, quarter), f32),
            jax.ShapeDtypeStruct((devices, ROWS, quarter), bf16),
        ),
        in_specs=[VMEM] * 7,
        out_specs=[VMEM] * 2,
        compiler_params=limit(12),
        name="mix",
    )(mine, near, far_y, far_both, hidden, route, gate_b)
    tokens = lax.all_to_all(spread, both, split_axis=0, concat_axis=0, tiled=True)
    parts = pl.pallas_call(
        functools.partial(expert_kernel, chunk),
        out_shape=jax.ShapeDtypeStruct((devices, ROWS, quarter), bf16),
        in_specs=[VMEM] * 6 + [ANY] * 3,
        out_specs=VMEM,
        scratch_shapes=[
            pltpu.VMEM((model // LANES, ROWS * req_count, LANES), f32),
            pltpu.VMEM((requests * req_count, 3 * EXPERTS), f32),
            pltpu.VMEM((requests * req_count, units), bf16),
            pltpu.VMEM((model // LANES, ROWS * req_count, LANES), f32),
            pltpu.VMEM((units - split_b, model), bf16),
            pltpu.VMEM((units - split_b, model), bf16),
            pltpu.VMEM((units, model), bf16),
            pltpu.SemaphoreType.DMA((2 * (units - split_b) // chunk + 3,)),
        ],
        compiler_params=limit(32),
        name="experts",
    )(tokens, gain, gate_a, up_a, gate_b, up_b, *on_hbm(gate, up, down_weight))
    parts = lax.all_to_all(parts, both, split_axis=0, concat_axis=0, tiled=True)
    return pl.pallas_call(
        final_kernel,
        out_shape=jax.ShapeDtypeStruct((requests, quarter), bf16),
        in_specs=[VMEM] * 2,
        out_specs=VMEM,
        compiler_params=limit(24),
        name="final",
    )(parts, mixed)


def solution(mesh):
    return jax.shard_map(
        per_device,
        mesh=mesh,
        in_specs=(
            P("req", None),
            P("req", "head", None),
            P(("req", "head"), None, None),
            P("req", None),
            P("req"),
            P("head", None, None),
            P("head", None),
            P(),
            P("req", None),
            P("req", None),
            P("req", None, "head"),
            P("req", None, "head"),
            P("req", "head", None),
        ),
        out_specs=P("req", "head"),
        check_vma=False,
    )
```

```python
import functools
import math

import jax
import jax.numpy as jnp
from jax import lax
from jax.experimental import pallas as pl
from jax.experimental.pallas import tpu as pltpu
from jax.sharding import PartitionSpec as P

RANK = 512
ROPE = 64
NOPE = 128
VHEAD = 128
EXPERTS = 64
TOP = 6
PAGE = 128
LANES = 128
ROWS = 8

norm_eps = 1e-06
masked_low = -1e30

f32 = jnp.float32
bf16 = jnp.bfloat16
NT = (((1,), (1,)), ((), ()))
VMEM = pl.BlockSpec(memory_space=pltpu.VMEM)
SMEM = pl.BlockSpec(memory_space=pltpu.SMEM)
ANY = pl.BlockSpec(memory_space=pl.ANY)


def split3(value):
    high = value.astype(bf16).astype(f32)
    rest = value - high
    middle = rest.astype(bf16).astype(f32)
    return high, middle, (rest - middle).astype(bf16).astype(f32)


def start_all(pairs, sems):
    copies = [
        pltpu.make_async_copy(src, dst, sems.at[n]) for n, (src, dst) in enumerate(pairs)
    ]
    for copy in copies:
        copy.start()
    return copies


def stage_kernel(*refs):
    table_in, lens_in, ids_in, mix_in = refs[:4]
    bias_out, route_out = refs[10:12]
    table, lens, ids, mix, small_sems, sems = refs[18:]
    small = start_all(
        ((table_in, table), (lens_in, lens), (ids_in, ids), (mix_in, mix)), small_sems
    )
    large = start_all(tuple(zip(refs[4:10], refs[12:18])), sems)
    for copy in small:
        copy.wait()
    head_at = lax.axis_index("head")
    width, requests = table.shape
    pages_here = bias_out.shape[0] // 2
    row_request = lax.broadcasted_iota(jnp.int32, bias_out.shape[1:], 0) // ROWS
    within = lax.broadcasted_iota(jnp.int32, bias_out.shape[1:], 1)
    for side in range(2):
        for p in range(pages_here):
            page = (head_at ^ side) * pages_here + p
            owner = jnp.int32(-1)
            count = jnp.int32(0)
            for r in range(requests):
                for m in range(width):
                    left = lens[r] - m * PAGE
                    hit = jnp.logical_and(table[m, r] == page, left > 0)
                    owner = jnp.where(hit, r, owner)
                    count = jnp.where(hit, left, count)
            valid = (row_request == owner) & (within < count)
            bias_out[side * pages_here + p] = jnp.where(valid, 1.0, 0.0)
    lanes = lax.broadcasted_iota(jnp.int32, route_out.shape, 1)
    row = jnp.zeros(route_out.shape, f32)
    for r in range(requests):
        for i in range(TOP):
            row = jnp.where(lanes == r * EXPERTS + ids[r, i], mix[r, i], row)
    high, middle, low = split3(row)
    route_out[...] = jnp.where(
        head_at == 0, high, jnp.where(head_at == 1, middle, jnp.where(head_at == 2, low, 0.0))
    )
    for copy in large:
        copy.wait()


def fetch_kernel(spans, *refs):
    count = len(spans)
    sources, outs, sems = refs[:count], refs[count + 1 : 2 * count + 1], refs[2 * count + 1]
    pairs = []
    for source, out, (first, last) in zip(sources, outs, spans):
        flat = source.reshape(source.shape[0] * source.shape[1], source.shape[2])
        pairs.append((flat.at[pl.ds(first, last - first), :], out))
    for copy in start_all(tuple(pairs), sems):
        copy.wait()


def attend_kernel(
    usable,
    q_own,
    q_far,
    cache_own,
    cache_near,
    own_out,
    own_lse,
    far_out,
    q_all,
    weighted,
    lse_all,
):
    requests, heads, width = q_own.shape
    pages_here = cache_own.shape[0]
    q_all[requests * ROWS :, :] = jnp.zeros((ROWS * (ROWS - requests), width), f32)
    for r in range(requests):
        q_all[r * ROWS : r * ROWS + heads, :] = q_own[r].astype(f32)
        q_all[r * ROWS + heads : r * ROWS + 2 * heads, :] = q_far[r].astype(f32)
    q_rows = q_all[...].astype(bf16)
    total_rows = q_all.shape[0]
    scale = 1.0 / math.sqrt(NOPE + ROPE)
    keys = [cache.at[p] for cache in (cache_own, cache_near) for p in range(pages_here)]
    valids = [usable[n] > 0.0 for n in range(2 * pages_here)]
    scores = []
    for key, valid in zip(keys, valids):
        score = jnp.dot(q_rows, key[...], preferred_element_type=f32) * scale
        scores.append(jnp.where(valid, score, masked_low))
    highest = functools.reduce(jnp.maximum, scores).max(axis=-1, keepdims=True)
    total = jnp.zeros((total_rows, 1), f32)
    summed = jnp.zeros((total_rows, RANK), f32)
    for key, valid, score in zip(keys, valids, scores):
        weight = jnp.where(valid, jnp.exp(score - highest), 0.0)
        total = total + jnp.sum(weight, axis=-1, keepdims=True)
        high = weight.astype(bf16)
        low = (weight - high.astype(f32)).astype(bf16)
        latent = key[:RANK, :]
        summed = summed + lax.dot_general(high, latent, NT, preferred_element_type=f32)
        summed = summed + lax.dot_general(low, latent, NT, preferred_element_type=f32)
    some = total > 0.0
    safe = jnp.where(some, total, 1.0)
    summed = summed * (1.0 / safe)
    for c in range(RANK // LANES):
        weighted[c] = summed[:, c * LANES : (c + 1) * LANES]
    lse = jnp.where(some, highest + jnp.log(safe), masked_low)
    lse_all[...] = jnp.broadcast_to(lse, lse_all.shape)
    lane = lax.broadcasted_iota(jnp.int32, (ROWS, LANES), 1)
    for h in range(heads):
        own_lse[h] = lse_all[pl.ds(h, ROWS, stride=ROWS), :]
        for c in range(RANK // LANES):
            span = slice(c * LANES, (c + 1) * LANES)
            own_out[h, :, span] = weighted[c, pl.ds(h, ROWS, stride=ROWS), :]
            far_out[h, :, span] = weighted[c, pl.ds(heads + h, ROWS, stride=ROWS), :].astype(bf16)
        high, middle, low = split3(lse_all[pl.ds(heads + h, ROWS, stride=ROWS), :])
        far_out[h, :, RANK:] = jnp.where(
            lane == 0, high, jnp.where(lane == 1, middle, jnp.where(lane == 2, low, 0.0))
        ).astype(bf16)


def project_kernel(own, own_lse, far, value_up, out_proj, _, mine, near, far_y, far_both, whole):
    heads = own.shape[0]
    head_at = lax.axis_index("head")
    parts = []
    for h in range(heads):
        stats = far[h, :, RANK:].astype(f32)
        lse_far = stats[:, 0:1] + stats[:, 1:2] + stats[:, 2:3]
        lse_own = own_lse[h][:, 0:1]
        highest = jnp.maximum(lse_own, lse_far)
        weight_own = jnp.exp(lse_own - highest)
        weight_far = jnp.exp(lse_far - highest)
        merged = weight_own * own[h] + weight_far * far[h, :, :RANK].astype(f32)
        attended = (merged * (1.0 / (weight_own + weight_far))).astype(bf16)
        parts.append(jnp.dot(attended, value_up[h], preferred_element_type=f32))
    head_out = jnp.concatenate(parts, axis=1).astype(bf16)
    whole[...] = jnp.dot(head_out, out_proj[...], preferred_element_type=f32)
    quarter = mine.shape[1]
    mine[...] = whole[:, pl.ds(pl.multiple_of(head_at * quarter, quarter), quarter)]
    for out, flip in ((near, 1), (far_y, 2), (far_both, 3)):
        start = pl.multiple_of((head_at ^ flip) * quarter, quarter)
        out[...] = whole[:, pl.ds(start, quarter)].astype(bf16)


def mix_kernel(mine, near, far_y, far_both, hidden, route, _, mixed_out, spread_out):
    head_at = lax.axis_index("head")
    requests = hidden.shape[0]
    quarter = mine.shape[1]
    start = pl.multiple_of(head_at * quarter, quarter)
    attn = mine[...] + near[...].astype(f32) + far_y[...].astype(f32) + far_both[...].astype(f32)
    residual = hidden[:, pl.ds(start, quarter)].astype(f32)
    mixed_out[...] = attn[:requests] + residual
    row = lax.broadcasted_iota(jnp.int32, (ROWS, quarter), 0)
    padded = jnp.concatenate(
        [residual, jnp.zeros((ROWS - requests, quarter), f32)], axis=0
    )
    block = jnp.where(row < requests, attn + padded, route[...]).astype(bf16)
    half = spread_out.shape[2]
    for n in range(spread_out.shape[0]):
        spread_out[n] = block[:, n % 2 * half : (n % 2 + 1) * half]


def chunk_groups(first, last, chunk, count):
    chunks = (last - first) // chunk
    edges = [first + chunks * n // count * chunk for n in range(count + 1)]
    return list(zip(edges, edges[1:]))


def expert_kernel(
    chunk,
    tokens,
    tokens_near,
    gain,
    gate_a,
    up_a,
    gate_b,
    up_b,
    gate_c,
    up_c,
    gate,
    up,
    down,
    out,
    rows_all,
    mix_all,
    active_all,
    total,
    gate_d,
    up_d,
    down_all,
    sems,
):
    req_count = lax.axis_size("req")
    head_count = lax.axis_size("head")
    req_at = lax.axis_index("req")
    slots, depth, model = down.shape
    quarter = model // head_count
    lower = lax.axis_index("head") % 2 == 0
    requests = ROWS - 1
    live = requests * req_count
    units = slots * depth
    ready = gate_a.shape[0] + gate_b.shape[0] + gate_c.shape[0]
    pairs = []
    halves = chunk_groups(ready, units, chunk, 2)
    for first, last in halves:
        for source, buffer in ((gate, gate_d), (up, up_d)):
            flat = source.reshape(units, model)
            pairs.append(
                (flat.at[pl.ds(first, last - first), :], buffer.at[pl.ds(first - ready, last - first), :])
            )
    groups = chunk_groups(0, units, chunk, 2)
    for first, last in groups:
        span = pl.ds(first, last - first)
        pairs.append((down.reshape(units, model).at[span, :], down_all.at[span, :]))
    loads = start_all(tuple(pairs), sems)
    for i in range(req_count):
        for j in range(head_count):
            here, there = (part[i * head_count + j].astype(f32) for part in (tokens, tokens_near))
            halves_of = (jnp.where(lower, here, there), jnp.where(lower, there, here))
            block = jnp.concatenate(halves_of, axis=1)
            for c in range(quarter // LANES):
                rows_all[j * quarter // LANES + c, pl.ds(i, ROWS, stride=req_count), :] = block[
                    :, c * LANES : (c + 1) * LANES
                ]
    for r in range(requests):
        for k in range(3):
            start = k * quarter + r * EXPERTS
            lane = start % LANES
            mix_all[r * req_count : (r + 1) * req_count, k * EXPERTS : (k + 1) * EXPERTS] = rows_all[
                start // LANES, live : live + req_count, lane : lane + EXPERTS
            ]
    mixed = jnp.concatenate([rows_all[c, :live, :] for c in range(model // LANES)], axis=1)
    spread = jnp.mean(mixed * mixed, axis=-1, keepdims=True)
    normed = (mixed * lax.rsqrt(spread + norm_eps) * gain[...]).astype(bf16)
    mix_rows = mix_all[...].astype(bf16)
    expert = lax.broadcasted_iota(jnp.int32, (max(slots, ROWS), 3 * EXPERTS), 1) % EXPERTS
    slot_at = req_at * slots + lax.broadcasted_iota(jnp.int32, expert.shape, 0)
    chosen = jnp.where(expert == slot_at // 2, 1.0, 0.0).astype(bf16)
    by_slot = lax.dot_general(chosen, mix_rows, NT, preferred_element_type=f32)
    homes = []
    for gate_at, up_at in ((gate_a, up_a), (gate_b, up_b), (gate_c, up_c), (gate_d, up_d)):
        homes += [(gate_at, up_at, offset) for offset in range(0, gate_at.shape[0], chunk)]
    for first, (gate_at, up_at, offset) in zip(range(0, units, chunk), homes):
        if first in [start for start, _ in halves]:
            loads.pop(0).wait()
            loads.pop(0).wait()
        unit = first + lax.broadcasted_iota(jnp.int32, (chunk, live), 0)
        weight = jnp.broadcast_to(by_slot[first // depth : first // depth + 1, :], (chunk, live))
        for slot in range(first // depth + 1, (first + chunk - 1) // depth + 1):
            weight = jnp.where(unit >= slot * depth, by_slot[slot : slot + 1, :], weight)
        gate_part = lax.dot_general(
            gate_at[offset : offset + chunk, :], normed, NT, preferred_element_type=f32
        )
        up_part = lax.dot_general(
            up_at[offset : offset + chunk, :], normed, NT, preferred_element_type=f32
        )
        active = gate_part / (1.0 + jnp.exp(-gate_part)) * up_part * weight
        active_all[:, first : first + chunk] = active.T.astype(bf16)
    for c in range(model // LANES):
        total[c, live:, :] = jnp.zeros((req_count, LANES), f32)
    for n, (first, last) in enumerate(groups):
        loads.pop(0).wait()
        product = jnp.dot(
            active_all[:, first:last], down_all[first:last, :], preferred_element_type=f32
        )
        for c in range(model // LANES):
            share = product[:, c * LANES : (c + 1) * LANES]
            total[c, :live, :] = share if n == 0 else total[c, :live, :] + share
    for i in range(req_count):
        for j in range(head_count):
            for c in range(quarter // LANES):
                out[i * head_count + j, :, c * LANES : (c + 1) * LANES] = total[
                    j * quarter // LANES + c, pl.ds(i, ROWS, stride=req_count), :
                ].astype(bf16)


def final_kernel(parts, mixed, out):
    total = jnp.sum(parts[...].astype(f32), axis=0)
    out[...] = (mixed[...] + total[: mixed.shape[0]]).astype(bf16)


def limit(mebibytes):
    return pltpu.CompilerParams(vmem_limit_bytes=mebibytes * 2**20)


def per_device(
    hidden,
    queries,
    latent_cache,
    page_table,
    seq_lens,
    value_up,
    out_proj,
    norm_gain,
    expert_ids,
    expert_mix,
    gate_weight,
    up_weight,
    down_weight,
):
    head_count = lax.axis_size("head")
    req_count = lax.axis_size("req")
    both = ("req", "head")
    requests, heads, width = queries.shape
    model = hidden.shape[1]
    quarter = model // head_count
    half = quarter // 2
    devices = req_count * head_count
    assert head_count == 4 and requests == ROWS - 1 and requests * EXPERTS <= quarter

    def swap(value, flip):
        return lax.ppermute(value, "head", [(n, n ^ flip) for n in range(head_count)])

    def on_hbm(*values):
        return [pltpu.with_memory_space_constraint(value, pltpu.HBM) for value in values]

    def fetch(after, *pieces):
        spans = tuple(span for _, span in pieces)
        shapes = tuple(pltpu.VMEM((last - first, model), bf16) for first, last in spans)
        size = sum(last - first for first, last in spans) * model * 2
        return pl.pallas_call(
            functools.partial(fetch_kernel, spans),
            out_shape=shapes,
            in_specs=[ANY] * (len(pieces) + 1),
            out_specs=[VMEM] * len(pieces),
            scratch_shapes=[pltpu.SemaphoreType.DMA((len(pieces),))],
            compiler_params=limit(4),
            cost_estimate=pl.CostEstimate(flops=0, bytes_accessed=size, transcendentals=0),
            name="fetch",
        )(*on_hbm(*(weight for weight, _ in pieces)), after)

    slots, _, depth = gate_weight.shape
    units = slots * depth
    chunk = units // 11
    split_a, split_b, split_c = 2 * chunk, 5 * chunk, 6 * chunk
    gate = jnp.swapaxes(gate_weight, 1, 2)
    up = jnp.swapaxes(up_weight, 1, 2)
    cache = jnp.swapaxes(latent_cache, 1, 2)
    pages_here = cache.shape[0]
    rows = ROWS * ROWS
    q_far = swap(queries, 2)
    cache_near = swap(cache, 1)
    large = (queries, cache, value_up, out_proj, hidden, norm_gain.reshape(1, model))
    usable, route, q_own, cache_own, value_up, out_proj, hidden, gain = pl.pallas_call(
        stage_kernel,
        out_shape=(
            pltpu.VMEM((2 * pages_here, rows, PAGE), f32),
            pltpu.VMEM((1, quarter), f32),
            *(pltpu.VMEM(value.shape, value.dtype) for value in large),
        ),
        in_specs=[ANY] * 10,
        out_specs=[VMEM] * 8,
        scratch_shapes=[
            pltpu.SMEM(page_table.shape[::-1], jnp.int32),
            pltpu.SMEM(seq_lens.shape, jnp.int32),
            pltpu.SMEM(expert_ids.shape, jnp.int32),
            pltpu.SMEM(expert_mix.shape, f32),
            pltpu.SemaphoreType.DMA((4,)),
            pltpu.SemaphoreType.DMA((6,)),
        ],
        compiler_params=limit(4),
        cost_estimate=pl.CostEstimate(flops=0, bytes_accessed=3 * 2**20, transcendentals=0),
        name="stage",
    )(*on_hbm(page_table.T, seq_lens, expert_ids, expert_mix, *large))
    own, own_lse, far = pl.pallas_call(
        attend_kernel,
        out_shape=(
            jax.ShapeDtypeStruct((heads, ROWS, RANK), f32),
            jax.ShapeDtypeStruct((heads, ROWS, LANES), f32),
            jax.ShapeDtypeStruct((heads, ROWS, RANK + LANES), bf16),
        ),
        in_specs=[VMEM] * 5,
        out_specs=[VMEM] * 3,
        scratch_shapes=[
            pltpu.VMEM((rows, width), f32),
            pltpu.VMEM((RANK // LANES, rows, LANES), f32),
            pltpu.VMEM((rows, LANES), f32),
        ],
        compiler_params=limit(8),
        name="attend",
    )(usable, q_own, q_far, cache_own, cache_near)
    gate_a, up_a = fetch(far, (gate, (0, split_a)), (up, (0, split_a)))
    far = swap(far, 2)
    piece = jax.ShapeDtypeStruct((ROWS, quarter), bf16)
    mine, near, far_y, far_both = pl.pallas_call(
        project_kernel,
        out_shape=(jax.ShapeDtypeStruct((ROWS, quarter), f32), piece, piece, piece),
        in_specs=[VMEM] * 6,
        out_specs=[VMEM] * 4,
        scratch_shapes=[pltpu.VMEM((ROWS, model), f32)],
        compiler_params=limit(8),
        name="project",
    )(own, own_lse, far, value_up, out_proj, gate_a)
    gate_b, up_b = fetch(near, (gate, (split_a, split_b)), (up, (split_a, split_b)))
    near, far_y, far_both = swap(near, 1), swap(far_y, 2), swap(far_both, 3)
    mixed, spread = pl.pallas_call(
        mix_kernel,
        out_shape=(
            jax.ShapeDtypeStruct((requests, quarter), f32),
            jax.ShapeDtypeStruct((devices, ROWS, half), bf16),
        ),
        in_specs=[VMEM] * 7,
        out_specs=[VMEM] * 2,
        compiler_params=limit(12),
        name="mix",
    )(mine, near, far_y, far_both, hidden, route, gate_b)
    tokens = lax.all_to_all(spread, both, split_axis=0, concat_axis=0, tiled=True)
    gate_c, up_c = fetch(tokens, (gate, (split_b, split_c)), (up, (split_b, split_c)))
    tokens_near = swap(tokens, 1)
    ready = (gate_a, up_a, gate_b, up_b, gate_c, up_c)
    parts = pl.pallas_call(
        functools.partial(expert_kernel, chunk),
        out_shape=jax.ShapeDtypeStruct((devices, ROWS, quarter), bf16),
        in_specs=[VMEM] * 9 + [ANY] * 3,
        out_specs=VMEM,
        scratch_shapes=[
            pltpu.VMEM((model // LANES, ROWS * req_count, LANES), f32),
            pltpu.VMEM((requests * req_count, 3 * EXPERTS), f32),
            pltpu.VMEM((requests * req_count, units), bf16),
            pltpu.VMEM((model // LANES, ROWS * req_count, LANES), f32),
            pltpu.VMEM((units - split_c, model), bf16),
            pltpu.VMEM((units - split_c, model), bf16),
            pltpu.VMEM((units, model), bf16),
            pltpu.SemaphoreType.DMA((6,)),
        ],
        compiler_params=limit(32),
        name="experts",
    )(tokens, tokens_near, gain, *ready, *on_hbm(gate, up, down_weight))
    parts = lax.all_to_all(parts, both, split_axis=0, concat_axis=0, tiled=True)
    return pl.pallas_call(
        final_kernel,
        out_shape=jax.ShapeDtypeStruct((requests, quarter), bf16),
        in_specs=[VMEM] * 2,
        out_specs=VMEM,
        compiler_params=limit(24),
        name="final",
    )(parts, mixed)


def solution(mesh):
    return jax.shard_map(
        per_device,
        mesh=mesh,
        in_specs=(
            P("req", None),
            P("req", "head", None),
            P(("req", "head"), None, None),
            P("req", None),
            P("req"),
            P("head", None, None),
            P("head", None),
            P(),
            P("req", None),
            P("req", None),
            P("req", None, "head"),
            P("req", None, "head"),
            P("req", "head", None),
        ),
        out_specs=P("req", "head"),
        check_vma=False,
    )
```

```python
import functools
import math

import jax
import jax.numpy as jnp
from jax import lax
from jax.experimental import pallas as pl
from jax.experimental.pallas import tpu as pltpu
from jax.sharding import PartitionSpec as P

RANK = 512
ROPE = 64
NOPE = 128
VHEAD = 128
EXPERTS = 64
TOP = 6
PAGE = 128
LANES = 128
ROWS = 8

norm_eps = 1e-06
masked_low = -1e30

f32 = jnp.float32
bf16 = jnp.bfloat16
NT = (((1,), (1,)), ((), ()))
VMEM = pl.BlockSpec(memory_space=pltpu.VMEM)
SMEM = pl.BlockSpec(memory_space=pltpu.SMEM)
ANY = pl.BlockSpec(memory_space=pl.ANY)


def split3(value):
    high = value.astype(bf16).astype(f32)
    rest = value - high
    middle = rest.astype(bf16).astype(f32)
    return high, middle, (rest - middle).astype(bf16).astype(f32)


def start_all(pairs, sems):
    copies = [
        pltpu.make_async_copy(src, dst, sems.at[n]) for n, (src, dst) in enumerate(pairs)
    ]
    for copy in copies:
        copy.start()
    return copies


def stage_kernel(*refs):
    table_in, lens_in, ids_in, mix_in = refs[:4]
    bias_out, route_out = refs[10:12]
    table, lens, ids, mix, small_sems, sems = refs[18:]
    small = start_all(
        ((table_in, table), (lens_in, lens), (ids_in, ids), (mix_in, mix)), small_sems
    )
    large = start_all(tuple(zip(refs[4:10], refs[12:18])), sems)
    for copy in small:
        copy.wait()
    head_at = lax.axis_index("head")
    width, requests = table.shape
    pages_here = bias_out.shape[0] // 2
    row_request = lax.broadcasted_iota(jnp.int32, bias_out.shape[1:], 0) // ROWS
    within = lax.broadcasted_iota(jnp.int32, bias_out.shape[1:], 1)
    for side in range(2):
        for p in range(pages_here):
            page = (head_at ^ side) * pages_here + p
            owner = jnp.int32(-1)
            count = jnp.int32(0)
            for r in range(requests):
                for m in range(width):
                    left = lens[r] - m * PAGE
                    hit = jnp.logical_and(table[m, r] == page, left > 0)
                    owner = jnp.where(hit, r, owner)
                    count = jnp.where(hit, left, count)
            valid = (row_request == owner) & (within < count)
            bias_out[side * pages_here + p] = jnp.where(valid, 1.0, 0.0)
    lanes = lax.broadcasted_iota(jnp.int32, route_out.shape, 1)
    row = jnp.zeros(route_out.shape, f32)
    for r in range(requests):
        for i in range(TOP):
            row = jnp.where(lanes == r * EXPERTS + ids[r, i], mix[r, i], row)
    high, middle, low = split3(row)
    route_out[...] = jnp.where(
        head_at == 0, high, jnp.where(head_at == 1, middle, jnp.where(head_at == 2, low, 0.0))
    )
    for copy in large:
        copy.wait()


def fetch_kernel(spans, *refs):
    count = len(spans)
    sources, outs, sems = refs[:count], refs[count + 1 : 2 * count + 1], refs[2 * count + 1]
    pairs = []
    for source, out, (first, last) in zip(sources, outs, spans):
        flat = source.reshape(source.shape[0] * source.shape[1], source.shape[2])
        pairs.append((flat.at[pl.ds(first, last - first), :], out))
    for copy in start_all(tuple(pairs), sems):
        copy.wait()


def attend_kernel(
    usable,
    q_own,
    q_far,
    cache_own,
    cache_near,
    own_out,
    own_lse,
    far_out,
    q_all,
    weighted,
    lse_all,
):
    requests, heads, width = q_own.shape
    pages_here = cache_own.shape[0]
    q_all[requests * ROWS :, :] = jnp.zeros((ROWS * (ROWS - requests), width), f32)
    for r in range(requests):
        q_all[r * ROWS : r * ROWS + heads, :] = q_own[r].astype(f32)
        q_all[r * ROWS + heads : r * ROWS + 2 * heads, :] = q_far[r].astype(f32)
    q_rows = q_all[...].astype(bf16)
    total_rows = q_all.shape[0]
    scale = 1.0 / math.sqrt(NOPE + ROPE)
    keys = [cache.at[p] for cache in (cache_own, cache_near) for p in range(pages_here)]
    valids = [usable[n] > 0.0 for n in range(2 * pages_here)]
    scores = []
    for key, valid in zip(keys, valids):
        score = jnp.dot(q_rows, key[...], preferred_element_type=f32) * scale
        scores.append(jnp.where(valid, score, masked_low))
    highest = functools.reduce(jnp.maximum, scores).max(axis=-1, keepdims=True)
    total = jnp.zeros((total_rows, 1), f32)
    summed = jnp.zeros((total_rows, RANK), f32)
    for key, valid, score in zip(keys, valids, scores):
        weight = jnp.where(valid, jnp.exp(score - highest), 0.0)
        total = total + jnp.sum(weight, axis=-1, keepdims=True)
        high = weight.astype(bf16)
        low = (weight - high.astype(f32)).astype(bf16)
        latent = key[:RANK, :]
        summed = summed + lax.dot_general(high, latent, NT, preferred_element_type=f32)
        summed = summed + lax.dot_general(low, latent, NT, preferred_element_type=f32)
    some = total > 0.0
    safe = jnp.where(some, total, 1.0)
    summed = summed * (1.0 / safe)
    for c in range(RANK // LANES):
        weighted[c] = summed[:, c * LANES : (c + 1) * LANES]
    lse = jnp.where(some, highest + jnp.log(safe), masked_low)
    lse_all[...] = jnp.broadcast_to(lse, lse_all.shape)
    lane = lax.broadcasted_iota(jnp.int32, (ROWS, LANES), 1)
    for h in range(heads):
        own_lse[h] = lse_all[pl.ds(h, ROWS, stride=ROWS), :]
        for c in range(RANK // LANES):
            span = slice(c * LANES, (c + 1) * LANES)
            own_out[h, :, span] = weighted[c, pl.ds(h, ROWS, stride=ROWS), :]
            far_out[h, :, span] = weighted[c, pl.ds(heads + h, ROWS, stride=ROWS), :].astype(bf16)
        high, middle, low = split3(lse_all[pl.ds(heads + h, ROWS, stride=ROWS), :])
        far_out[h, :, RANK:] = jnp.where(
            lane == 0, high, jnp.where(lane == 1, middle, jnp.where(lane == 2, low, 0.0))
        ).astype(bf16)


def project_kernel(own, own_lse, far, value_up, out_proj, _, mine, near, far_y, far_both, whole):
    heads = own.shape[0]
    head_at = lax.axis_index("head")
    parts = []
    for h in range(heads):
        stats = far[h, :, RANK:].astype(f32)
        lse_far = stats[:, 0:1] + stats[:, 1:2] + stats[:, 2:3]
        lse_own = own_lse[h][:, 0:1]
        highest = jnp.maximum(lse_own, lse_far)
        weight_own = jnp.exp(lse_own - highest)
        weight_far = jnp.exp(lse_far - highest)
        merged = weight_own * own[h] + weight_far * far[h, :, :RANK].astype(f32)
        attended = (merged * (1.0 / (weight_own + weight_far))).astype(bf16)
        parts.append(jnp.dot(attended, value_up[h], preferred_element_type=f32))
    head_out = jnp.concatenate(parts, axis=1).astype(bf16)
    whole[...] = jnp.dot(head_out, out_proj[...], preferred_element_type=f32)
    quarter = mine.shape[1]
    mine[...] = whole[:, pl.ds(pl.multiple_of(head_at * quarter, quarter), quarter)]
    for out, flip in ((near, 1), (far_y, 2), (far_both, 3)):
        start = pl.multiple_of((head_at ^ flip) * quarter, quarter)
        out[...] = whole[:, pl.ds(start, quarter)].astype(bf16)


def mix_kernel(mine, near, far_y, far_both, hidden, route, _, mixed_out, spread_out):
    head_at = lax.axis_index("head")
    requests = hidden.shape[0]
    quarter = mine.shape[1]
    start = pl.multiple_of(head_at * quarter, quarter)
    attn = mine[...] + near[...].astype(f32) + far_y[...].astype(f32) + far_both[...].astype(f32)
    residual = hidden[:, pl.ds(start, quarter)].astype(f32)
    mixed_out[...] = attn[:requests] + residual
    row = lax.broadcasted_iota(jnp.int32, (ROWS, quarter), 0)
    padded = jnp.concatenate(
        [residual, jnp.zeros((ROWS - requests, quarter), f32)], axis=0
    )
    block = jnp.where(row < requests, attn + padded, route[...]).astype(bf16)
    half = spread_out.shape[2]
    for n in range(spread_out.shape[0]):
        spread_out[n] = block[:, n % 2 * half : (n % 2 + 1) * half]


def chunk_groups(first, last, chunk, count):
    chunks = (last - first) // chunk
    edges = [first + chunks * n // count * chunk for n in range(count + 1)]
    return list(zip(edges, edges[1:]))


def expert_kernel(
    chunk,
    tokens,
    tokens_near,
    gain,
    gate_a,
    up_a,
    gate_b,
    up_b,
    gate_c,
    up_c,
    gate,
    up,
    down,
    theirs_out,
    active_out,
    down_own,
    rows_all,
    mix_all,
    active_all,
    total,
    gate_d,
    up_d,
    down_theirs,
    sems,
):
    req_count = lax.axis_size("req")
    head_count = lax.axis_size("head")
    req_at = lax.axis_index("req")
    slots, depth, model = down.shape
    quarter = model // head_count
    lower = lax.axis_index("head") % 2 == 0
    requests = ROWS - 1
    live = requests * req_count
    units = slots * depth
    ready = gate_a.shape[0] + gate_b.shape[0] + gate_c.shape[0]
    pairs = []
    halves = chunk_groups(ready, units, chunk, 1)
    for first, last in halves:
        for source, buffer in ((gate, gate_d), (up, up_d)):
            flat = source.reshape(units, model)
            pairs.append(
                (flat.at[pl.ds(first, last - first), :], buffer.at[pl.ds(first - ready, last - first), :])
            )
    half = quarter // 2
    flat = down.reshape(units, model)
    for buffer, at in ((down_theirs, jnp.where(lower, 1, 0)), (down_own, jnp.where(lower, 0, 1))):
        for j in range(head_count):
            start = pl.multiple_of((2 * j + at) * half, half)
            pairs.append((flat.at[:, pl.ds(start, half)], buffer.at[:, pl.ds(j * half, half)]))
    loads = start_all(tuple(pairs), sems)
    for i in range(req_count):
        for j in range(head_count):
            here, there = (part[i * head_count + j].astype(f32) for part in (tokens, tokens_near))
            halves_of = (jnp.where(lower, here, there), jnp.where(lower, there, here))
            block = jnp.concatenate(halves_of, axis=1)
            for c in range(quarter // LANES):
                rows_all[j * quarter // LANES + c, pl.ds(i, ROWS, stride=req_count), :] = block[
                    :, c * LANES : (c + 1) * LANES
                ]
    for r in range(requests):
        for k in range(3):
            start = k * quarter + r * EXPERTS
            lane = start % LANES
            mix_all[r * req_count : (r + 1) * req_count, k * EXPERTS : (k + 1) * EXPERTS] = rows_all[
                start // LANES, live : live + req_count, lane : lane + EXPERTS
            ]
    mixed = jnp.concatenate([rows_all[c, :live, :] for c in range(model // LANES)], axis=1)
    spread = jnp.mean(mixed * mixed, axis=-1, keepdims=True)
    normed = (mixed * lax.rsqrt(spread + norm_eps) * gain[...]).astype(bf16)
    mix_rows = mix_all[...].astype(bf16)
    expert = lax.broadcasted_iota(jnp.int32, (max(slots, ROWS), 3 * EXPERTS), 1) % EXPERTS
    slot_at = req_at * slots + lax.broadcasted_iota(jnp.int32, expert.shape, 0)
    chosen = jnp.where(expert == slot_at // 2, 1.0, 0.0).astype(bf16)
    by_slot = lax.dot_general(chosen, mix_rows, NT, preferred_element_type=f32)
    homes = []
    for gate_at, up_at in ((gate_a, up_a), (gate_b, up_b), (gate_c, up_c), (gate_d, up_d)):
        homes += [(gate_at, up_at, offset) for offset in range(0, gate_at.shape[0], chunk)]
    for first, (gate_at, up_at, offset) in zip(range(0, units, chunk), homes):
        if first in [start for start, _ in halves]:
            loads.pop(0).wait()
            loads.pop(0).wait()
        unit = first + lax.broadcasted_iota(jnp.int32, (chunk, live), 0)
        weight = jnp.broadcast_to(by_slot[first // depth : first // depth + 1, :], (chunk, live))
        for slot in range(first // depth + 1, (first + chunk - 1) // depth + 1):
            weight = jnp.where(unit >= slot * depth, by_slot[slot : slot + 1, :], weight)
        gate_part = lax.dot_general(
            gate_at[offset : offset + chunk, :], normed, NT, preferred_element_type=f32
        )
        up_part = lax.dot_general(
            up_at[offset : offset + chunk, :], normed, NT, preferred_element_type=f32
        )
        active = gate_part / (1.0 + jnp.exp(-gate_part)) * up_part * weight
        active_all[:, first : first + chunk] = active.T.astype(bf16)
    for _ in range(head_count):
        loads.pop(0).wait()
    active_out[...] = active_all[...]
    down_half(active_all, down_theirs, theirs_out, total)
    for load in loads:
        load.wait()


def down_half(active, weights, out, total):
    groups, rows, _ = total.shape
    live = active.shape[0]
    req_count = rows // ROWS
    head_count = out.shape[0] // req_count
    product = jnp.dot(active[...], weights[...], preferred_element_type=f32)
    for c in range(groups):
        total[c, :live, :] = product[:, c * LANES : (c + 1) * LANES]
        total[c, live:, :] = jnp.zeros((req_count, LANES), f32)
    wide = groups // head_count
    for i in range(req_count):
        for j in range(head_count):
            for c in range(wide):
                out[i * head_count + j, :, c * LANES : (c + 1) * LANES] = total[
                    j * wide + c, pl.ds(i, ROWS, stride=req_count), :
                ].astype(out.dtype)


def join_kernel(mine, theirs, out):
    out[...] = (mine[...] + theirs[...].astype(f32)).astype(bf16)


def final_kernel(parts, mixed, out):
    halves = []
    for side in range(2):
        sources = [parts[n].astype(f32) for n in range(side, parts.shape[0], 2)]
        halves.append(functools.reduce(jnp.add, sources))
    total = jnp.concatenate(halves, axis=1)
    out[...] = (mixed[...] + total[: mixed.shape[0]]).astype(bf16)


def limit(mebibytes):
    return pltpu.CompilerParams(vmem_limit_bytes=mebibytes * 2**20)


def per_device(
    hidden,
    queries,
    latent_cache,
    page_table,
    seq_lens,
    value_up,
    out_proj,
    norm_gain,
    expert_ids,
    expert_mix,
    gate_weight,
    up_weight,
    down_weight,
):
    head_count = lax.axis_size("head")
    req_count = lax.axis_size("req")
    both = ("req", "head")
    requests, heads, width = queries.shape
    model = hidden.shape[1]
    quarter = model // head_count
    half = quarter // 2
    devices = req_count * head_count
    assert head_count == 4 and requests == ROWS - 1 and requests * EXPERTS <= quarter

    def swap(value, flip):
        return lax.ppermute(value, "head", [(n, n ^ flip) for n in range(head_count)])

    def on_hbm(*values):
        return [pltpu.with_memory_space_constraint(value, pltpu.HBM) for value in values]

    def fetch(after, *pieces):
        spans = tuple(span for _, span in pieces)
        shapes = tuple(pltpu.VMEM((last - first, model), bf16) for first, last in spans)
        size = sum(last - first for first, last in spans) * model * 2
        return pl.pallas_call(
            functools.partial(fetch_kernel, spans),
            out_shape=shapes,
            in_specs=[ANY] * (len(pieces) + 1),
            out_specs=[VMEM] * len(pieces),
            scratch_shapes=[pltpu.SemaphoreType.DMA((len(pieces),))],
            compiler_params=limit(4),
            cost_estimate=pl.CostEstimate(flops=0, bytes_accessed=size, transcendentals=0),
            name="fetch",
        )(*on_hbm(*(weight for weight, _ in pieces)), after)

    slots, _, depth = gate_weight.shape
    units = slots * depth
    chunk = units // 11
    split_a, split_b, split_c = 2 * chunk, 5 * chunk, 6 * chunk
    gate = jnp.swapaxes(gate_weight, 1, 2)
    up = jnp.swapaxes(up_weight, 1, 2)
    cache = jnp.swapaxes(latent_cache, 1, 2)
    pages_here = cache.shape[0]
    rows = ROWS * ROWS
    q_far = swap(queries, 2)
    cache_near = swap(cache, 1)
    large = (queries, cache, value_up, out_proj, hidden, norm_gain.reshape(1, model))
    usable, route, q_own, cache_own, value_up, out_proj, hidden, gain = pl.pallas_call(
        stage_kernel,
        out_shape=(
            pltpu.VMEM((2 * pages_here, rows, PAGE), f32),
            pltpu.VMEM((1, quarter), f32),
            *(pltpu.VMEM(value.shape, value.dtype) for value in large),
        ),
        in_specs=[ANY] * 10,
        out_specs=[VMEM] * 8,
        scratch_shapes=[
            pltpu.SMEM(page_table.shape[::-1], jnp.int32),
            pltpu.SMEM(seq_lens.shape, jnp.int32),
            pltpu.SMEM(expert_ids.shape, jnp.int32),
            pltpu.SMEM(expert_mix.shape, f32),
            pltpu.SemaphoreType.DMA((4,)),
            pltpu.SemaphoreType.DMA((6,)),
        ],
        compiler_params=limit(4),
        cost_estimate=pl.CostEstimate(flops=0, bytes_accessed=3 * 2**20, transcendentals=0),
        name="stage",
    )(*on_hbm(page_table.T, seq_lens, expert_ids, expert_mix, *large))
    own, own_lse, far = pl.pallas_call(
        attend_kernel,
        out_shape=(
            jax.ShapeDtypeStruct((heads, ROWS, RANK), f32),
            jax.ShapeDtypeStruct((heads, ROWS, LANES), f32),
            jax.ShapeDtypeStruct((heads, ROWS, RANK + LANES), bf16),
        ),
        in_specs=[VMEM] * 5,
        out_specs=[VMEM] * 3,
        scratch_shapes=[
            pltpu.VMEM((rows, width), f32),
            pltpu.VMEM((RANK // LANES, rows, LANES), f32),
            pltpu.VMEM((rows, LANES), f32),
        ],
        compiler_params=limit(8),
        name="attend",
    )(usable, q_own, q_far, cache_own, cache_near)
    gate_a, up_a = fetch(far, (gate, (0, split_a)), (up, (0, split_a)))
    far = swap(far, 2)
    piece = jax.ShapeDtypeStruct((ROWS, quarter), bf16)
    mine, near, far_y, far_both = pl.pallas_call(
        project_kernel,
        out_shape=(jax.ShapeDtypeStruct((ROWS, quarter), f32), piece, piece, piece),
        in_specs=[VMEM] * 6,
        out_specs=[VMEM] * 4,
        scratch_shapes=[pltpu.VMEM((ROWS, model), f32)],
        compiler_params=limit(8),
        name="project",
    )(own, own_lse, far, value_up, out_proj, gate_a)
    gate_b, up_b = fetch(near, (gate, (split_a, split_b)), (up, (split_a, split_b)))
    near, far_y, far_both = swap(near, 1), swap(far_y, 2), swap(far_both, 3)
    mixed, spread = pl.pallas_call(
        mix_kernel,
        out_shape=(
            jax.ShapeDtypeStruct((requests, quarter), f32),
            jax.ShapeDtypeStruct((devices, ROWS, half), bf16),
        ),
        in_specs=[VMEM] * 7,
        out_specs=[VMEM] * 2,
        compiler_params=limit(12),
        name="mix",
    )(mine, near, far_y, far_both, hidden, route, gate_b)
    tokens = lax.all_to_all(spread, both, split_axis=0, concat_axis=0, tiled=True)
    gate_c, up_c = fetch(tokens, (gate, (split_b, split_c)), (up, (split_b, split_c)))
    tokens_near = swap(tokens, 1)
    ready = (gate_a, up_a, gate_b, up_b, gate_c, up_c)
    theirs, active, down_own = pl.pallas_call(
        functools.partial(expert_kernel, chunk),
        out_shape=(
            jax.ShapeDtypeStruct((devices, ROWS, half), bf16),
            pltpu.VMEM((requests * req_count, units), bf16),
            pltpu.VMEM((units, model // 2), bf16),
        ),
        in_specs=[VMEM] * 9 + [ANY] * 3,
        out_specs=[VMEM] * 3,
        scratch_shapes=[
            pltpu.VMEM((model // LANES, ROWS * req_count, LANES), f32),
            pltpu.VMEM((requests * req_count, 3 * EXPERTS), f32),
            pltpu.VMEM((requests * req_count, units), bf16),
            pltpu.VMEM((model // 2 // LANES, ROWS * req_count, LANES), f32),
            pltpu.VMEM((units - split_c, model), bf16),
            pltpu.VMEM((units - split_c, model), bf16),
            pltpu.VMEM((units, model // 2), bf16),
            pltpu.SemaphoreType.DMA((2 + 2 * head_count,)),
        ],
        compiler_params=limit(32),
        name="experts",
    )(tokens, tokens_near, gain, *ready, *on_hbm(gate, up, down_weight))
    mine_half = pl.pallas_call(
        down_half,
        out_shape=jax.ShapeDtypeStruct((devices, ROWS, half), f32),
        in_specs=[VMEM] * 2,
        out_specs=VMEM,
        scratch_shapes=[pltpu.VMEM((model // 2 // LANES, ROWS * req_count, LANES), f32)],
        compiler_params=limit(12),
        cost_estimate=pl.CostEstimate(
            flops=2 * requests * req_count * units * model, bytes_accessed=units * model, transcendentals=0
        ),
        name="down",
    )(active, down_own)
    parts = pl.pallas_call(
        join_kernel,
        out_shape=jax.ShapeDtypeStruct((devices, ROWS, half), bf16),
        in_specs=[VMEM] * 2,
        out_specs=VMEM,
        compiler_params=limit(12),
        name="join",
    )(mine_half, swap(theirs, 1))
    parts = lax.all_to_all(parts, both, split_axis=0, concat_axis=0, tiled=True)
    return pl.pallas_call(
        final_kernel,
        out_shape=jax.ShapeDtypeStruct((requests, quarter), bf16),
        in_specs=[VMEM] * 2,
        out_specs=VMEM,
        compiler_params=limit(24),
        name="final",
    )(parts, mixed)


def solution(mesh):
    return jax.shard_map(
        per_device,
        mesh=mesh,
        in_specs=(
            P("req", None),
            P("req", "head", None),
            P(("req", "head"), None, None),
            P("req", None),
            P("req"),
            P("head", None, None),
            P("head", None),
            P(),
            P("req", None),
            P("req", None),
            P("req", None, "head"),
            P("req", None, "head"),
            P("req", "head", None),
        ),
        out_specs=P("req", "head"),
        check_vma=False,
    )
```

```python
import functools
import math

import jax
import jax.numpy as jnp
from jax import lax
from jax.experimental import pallas as pl
from jax.experimental.pallas import tpu as pltpu
from jax.sharding import PartitionSpec as P

RANK = 512
ROPE = 64
NOPE = 128
VHEAD = 128
EXPERTS = 64
TOP = 6
PAGE = 128
LANES = 128
ROWS = 8

norm_eps = 1e-06
masked_low = -1e30

f32 = jnp.float32
bf16 = jnp.bfloat16
NT = (((1,), (1,)), ((), ()))
VMEM = pl.BlockSpec(memory_space=pltpu.VMEM)
SMEM = pl.BlockSpec(memory_space=pltpu.SMEM)
ANY = pl.BlockSpec(memory_space=pl.ANY)


def split3(value):
    high = value.astype(bf16).astype(f32)
    rest = value - high
    middle = rest.astype(bf16).astype(f32)
    return high, middle, (rest - middle).astype(bf16).astype(f32)


def start_all(pairs, sems):
    copies = [
        pltpu.make_async_copy(src, dst, sems.at[n]) for n, (src, dst) in enumerate(pairs)
    ]
    for copy in copies:
        copy.start()
    return copies


def stage_kernel(*refs):
    table_in, lens_in, ids_in, mix_in = refs[:4]
    bias_out, route_out = refs[10:12]
    table, lens, ids, mix, small_sems, sems = refs[18:]
    small = start_all(
        ((table_in, table), (lens_in, lens), (ids_in, ids), (mix_in, mix)), small_sems
    )
    large = start_all(tuple(zip(refs[4:10], refs[12:18])), sems)
    for copy in small:
        copy.wait()
    head_at = lax.axis_index("head")
    width, requests = table.shape
    pages_here = bias_out.shape[0] // 2
    row_request = lax.broadcasted_iota(jnp.int32, bias_out.shape[1:], 0) // ROWS
    within = lax.broadcasted_iota(jnp.int32, bias_out.shape[1:], 1)
    for side in range(2):
        for p in range(pages_here):
            page = (head_at ^ side) * pages_here + p
            owner = jnp.int32(-1)
            count = jnp.int32(0)
            for r in range(requests):
                for m in range(width):
                    left = lens[r] - m * PAGE
                    hit = jnp.logical_and(table[m, r] == page, left > 0)
                    owner = jnp.where(hit, r, owner)
                    count = jnp.where(hit, left, count)
            valid = (row_request == owner) & (within < count)
            bias_out[side * pages_here + p] = jnp.where(valid, 1.0, 0.0)
    lanes = lax.broadcasted_iota(jnp.int32, route_out.shape, 1)
    row = jnp.zeros(route_out.shape, f32)
    for r in range(requests):
        for i in range(TOP):
            row = jnp.where(lanes == r * EXPERTS + ids[r, i], mix[r, i], row)
    high, middle, low = split3(row)
    route_out[...] = jnp.where(
        head_at == 0, high, jnp.where(head_at == 1, middle, jnp.where(head_at == 2, low, 0.0))
    )
    for copy in large:
        copy.wait()


def fetch_kernel(spans, *refs):
    count = len(spans)
    sources, outs, sems = refs[:count], refs[count + 1 : 2 * count + 1], refs[2 * count + 1]
    pairs = []
    for source, out, (first, last) in zip(sources, outs, spans):
        flat = source.reshape(source.shape[0] * source.shape[1], source.shape[2])
        pairs.append((flat.at[pl.ds(first, last - first), :], out))
    for copy in start_all(tuple(pairs), sems):
        copy.wait()


def attend_kernel(
    usable,
    q_own,
    q_far,
    cache_own,
    cache_near,
    own_out,
    own_lse,
    far_out,
    q_all,
    weighted,
    lse_all,
):
    requests, heads, width = q_own.shape
    pages_here = cache_own.shape[0]
    q_all[requests * ROWS :, :] = jnp.zeros((ROWS * (ROWS - requests), width), f32)
    for r in range(requests):
        q_all[r * ROWS : r * ROWS + heads, :] = q_own[r].astype(f32)
        q_all[r * ROWS + heads : r * ROWS + 2 * heads, :] = q_far[r].astype(f32)
    q_rows = q_all[...].astype(bf16)
    total_rows = q_all.shape[0]
    scale = 1.0 / math.sqrt(NOPE + ROPE)
    keys = [cache.at[p] for cache in (cache_own, cache_near) for p in range(pages_here)]
    valids = [usable[n] > 0.0 for n in range(2 * pages_here)]
    scores = []
    for key, valid in zip(keys, valids):
        score = jnp.dot(q_rows, key[...], preferred_element_type=f32) * scale
        scores.append(jnp.where(valid, score, masked_low))
    highest = functools.reduce(jnp.maximum, scores).max(axis=-1, keepdims=True)
    total = jnp.zeros((total_rows, 1), f32)
    summed = jnp.zeros((total_rows, RANK), f32)
    for key, valid, score in zip(keys, valids, scores):
        weight = jnp.where(valid, jnp.exp(score - highest), 0.0)
        total = total + jnp.sum(weight, axis=-1, keepdims=True)
        high = weight.astype(bf16)
        low = (weight - high.astype(f32)).astype(bf16)
        latent = key[:RANK, :]
        summed = summed + lax.dot_general(high, latent, NT, preferred_element_type=f32)
        summed = summed + lax.dot_general(low, latent, NT, preferred_element_type=f32)
    some = total > 0.0
    safe = jnp.where(some, total, 1.0)
    summed = summed * (1.0 / safe)
    for c in range(RANK // LANES):
        weighted[c] = summed[:, c * LANES : (c + 1) * LANES]
    lse = jnp.where(some, highest + jnp.log(safe), masked_low)
    lse_all[...] = jnp.broadcast_to(lse, lse_all.shape)
    lane = lax.broadcasted_iota(jnp.int32, (ROWS, LANES), 1)
    for h in range(heads):
        own_lse[h] = lse_all[pl.ds(h, ROWS, stride=ROWS), :]
        for c in range(RANK // LANES):
            span = slice(c * LANES, (c + 1) * LANES)
            own_out[h, :, span] = weighted[c, pl.ds(h, ROWS, stride=ROWS), :]
            far_out[h, :, span] = weighted[c, pl.ds(heads + h, ROWS, stride=ROWS), :].astype(bf16)
        high, middle, low = split3(lse_all[pl.ds(heads + h, ROWS, stride=ROWS), :])
        far_out[h, :, RANK:] = jnp.where(
            lane == 0, high, jnp.where(lane == 1, middle, jnp.where(lane == 2, low, 0.0))
        ).astype(bf16)


def project_kernel(own, own_lse, far, value_up, out_proj, _, mine, near, far_y, far_both, whole):
    heads = own.shape[0]
    head_at = lax.axis_index("head")
    parts = []
    for h in range(heads):
        stats = far[h, :, RANK:].astype(f32)
        lse_far = stats[:, 0:1] + stats[:, 1:2] + stats[:, 2:3]
        lse_own = own_lse[h][:, 0:1]
        highest = jnp.maximum(lse_own, lse_far)
        weight_own = jnp.exp(lse_own - highest)
        weight_far = jnp.exp(lse_far - highest)
        merged = weight_own * own[h] + weight_far * far[h, :, :RANK].astype(f32)
        attended = (merged * (1.0 / (weight_own + weight_far))).astype(bf16)
        parts.append(jnp.dot(attended, value_up[h], preferred_element_type=f32))
    head_out = jnp.concatenate(parts, axis=1).astype(bf16)
    whole[...] = jnp.dot(head_out, out_proj[...], preferred_element_type=f32)
    quarter = mine.shape[1]
    mine[...] = whole[:, pl.ds(pl.multiple_of(head_at * quarter, quarter), quarter)]
    for out, flip in ((near, 1), (far_y, 2), (far_both, 3)):
        start = pl.multiple_of((head_at + flip) % 4 * quarter, quarter)
        out[...] = whole[:, pl.ds(start, quarter)].astype(bf16)


def mix_kernel(mine, near, far_y, far_both, hidden, route, _, mixed_out, spread_out):
    head_at = lax.axis_index("head")
    requests = hidden.shape[0]
    quarter = mine.shape[1]
    start = pl.multiple_of(head_at * quarter, quarter)
    attn = mine[...] + near[...].astype(f32) + far_y[...].astype(f32) + far_both[...].astype(f32)
    residual = hidden[:, pl.ds(start, quarter)].astype(f32)
    mixed_out[...] = attn[:requests] + residual
    row = lax.broadcasted_iota(jnp.int32, (ROWS, quarter), 0)
    padded = jnp.concatenate(
        [residual, jnp.zeros((ROWS - requests, quarter), f32)], axis=0
    )
    block = jnp.where(row < requests, attn + padded, route[...]).astype(bf16)
    half = spread_out.shape[2]
    for n in range(spread_out.shape[0]):
        spread_out[n] = block[:, n % 2 * half : (n % 2 + 1) * half]


def chunk_groups(first, last, chunk, count):
    chunks = (last - first) // chunk
    edges = [first + chunks * n // count * chunk for n in range(count + 1)]
    return list(zip(edges, edges[1:]))


def expert_kernel(
    chunk,
    tokens,
    tokens_near,
    gain,
    gate_a,
    up_a,
    gate_b,
    up_b,
    gate_c,
    up_c,
    gate,
    up,
    down,
    theirs_out,
    active_out,
    down_own,
    rows_all,
    mix_all,
    active_all,
    total,
    gate_d,
    up_d,
    down_theirs,
    sems,
):
    req_count = lax.axis_size("req")
    head_count = lax.axis_size("head")
    req_at = lax.axis_index("req")
    slots, depth, model = down.shape
    quarter = model // head_count
    lower = lax.axis_index("head") % 2 == 0
    requests = ROWS - 1
    live = requests * req_count
    units = slots * depth
    ready = gate_a.shape[0] + gate_b.shape[0] + gate_c.shape[0]
    pairs = []
    halves = chunk_groups(ready, units, chunk, 1)
    for first, last in halves:
        for source, buffer in ((gate, gate_d), (up, up_d)):
            flat = source.reshape(units, model)
            pairs.append(
                (flat.at[pl.ds(first, last - first), :], buffer.at[pl.ds(first - ready, last - first), :])
            )
    half = quarter // 2
    flat = down.reshape(units, model)
    for buffer, at in ((down_theirs, jnp.where(lower, 1, 0)), (down_own, jnp.where(lower, 0, 1))):
        for j in range(head_count):
            start = pl.multiple_of((2 * j + at) * half, half)
            pairs.append((flat.at[:, pl.ds(start, half)], buffer.at[:, pl.ds(j * half, half)]))
    loads = start_all(tuple(pairs), sems)
    for i in range(req_count):
        for j in range(head_count):
            here, there = (part[i * head_count + j].astype(f32) for part in (tokens, tokens_near))
            halves_of = (jnp.where(lower, here, there), jnp.where(lower, there, here))
            block = jnp.concatenate(halves_of, axis=1)
            for c in range(quarter // LANES):
                rows_all[j * quarter // LANES + c, pl.ds(i, ROWS, stride=req_count), :] = block[
                    :, c * LANES : (c + 1) * LANES
                ]
    for r in range(requests):
        for k in range(3):
            start = k * quarter + r * EXPERTS
            lane = start % LANES
            mix_all[r * req_count : (r + 1) * req_count, k * EXPERTS : (k + 1) * EXPERTS] = rows_all[
                start // LANES, live : live + req_count, lane : lane + EXPERTS
            ]
    mixed = jnp.concatenate([rows_all[c, :live, :] for c in range(model // LANES)], axis=1)
    spread = jnp.mean(mixed * mixed, axis=-1, keepdims=True)
    normed = (mixed * lax.rsqrt(spread + norm_eps) * gain[...]).astype(bf16)
    mix_rows = mix_all[...].astype(bf16)
    expert = lax.broadcasted_iota(jnp.int32, (max(slots, ROWS), 3 * EXPERTS), 1) % EXPERTS
    slot_at = req_at * slots + lax.broadcasted_iota(jnp.int32, expert.shape, 0)
    chosen = jnp.where(expert == slot_at // 2, 1.0, 0.0).astype(bf16)
    by_slot = lax.dot_general(chosen, mix_rows, NT, preferred_element_type=f32)
    homes = []
    for gate_at, up_at in ((gate_a, up_a), (gate_b, up_b), (gate_c, up_c), (gate_d, up_d)):
        homes += [(gate_at, up_at, offset) for offset in range(0, gate_at.shape[0], chunk)]
    for first, (gate_at, up_at, offset) in zip(range(0, units, chunk), homes):
        if first in [start for start, _ in halves]:
            loads.pop(0).wait()
            loads.pop(0).wait()
        unit = first + lax.broadcasted_iota(jnp.int32, (chunk, live), 0)
        weight = jnp.broadcast_to(by_slot[first // depth : first // depth + 1, :], (chunk, live))
        for slot in range(first // depth + 1, (first + chunk - 1) // depth + 1):
            weight = jnp.where(unit >= slot * depth, by_slot[slot : slot + 1, :], weight)
        gate_part = lax.dot_general(
            gate_at[offset : offset + chunk, :], normed, NT, preferred_element_type=f32
        )
        up_part = lax.dot_general(
            up_at[offset : offset + chunk, :], normed, NT, preferred_element_type=f32
        )
        active = gate_part / (1.0 + jnp.exp(-gate_part)) * up_part * weight
        active_all[:, first : first + chunk] = active.T.astype(bf16)
    for _ in range(head_count):
        loads.pop(0).wait()
    active_out[...] = active_all[...]
    down_half(active_all, down_theirs, theirs_out, total)
    for load in loads:
        load.wait()


def down_half(active, weights, out, total):
    groups, rows, _ = total.shape
    live = active.shape[0]
    req_count = rows // ROWS
    head_count = out.shape[0] // req_count
    product = jnp.dot(active[...], weights[...], preferred_element_type=f32)
    for c in range(groups):
        total[c, :live, :] = product[:, c * LANES : (c + 1) * LANES]
        total[c, live:, :] = jnp.zeros((req_count, LANES), f32)
    wide = groups // head_count
    for i in range(req_count):
        for j in range(head_count):
            for c in range(wide):
                out[i * head_count + j, :, c * LANES : (c + 1) * LANES] = total[
                    j * wide + c, pl.ds(i, ROWS, stride=req_count), :
                ].astype(out.dtype)


def join_kernel(mine, theirs, out):
    out[...] = (mine[...] + theirs[...].astype(f32)).astype(bf16)


def final_kernel(parts, mixed, out):
    halves = []
    for side in range(2):
        sources = [parts[n].astype(f32) for n in range(side, parts.shape[0], 2)]
        halves.append(functools.reduce(jnp.add, sources))
    total = jnp.concatenate(halves, axis=1)
    out[...] = (mixed[...] + total[: mixed.shape[0]]).astype(bf16)


def limit(mebibytes):
    return pltpu.CompilerParams(vmem_limit_bytes=mebibytes * 2**20)


def per_device(
    hidden,
    queries,
    latent_cache,
    page_table,
    seq_lens,
    value_up,
    out_proj,
    norm_gain,
    expert_ids,
    expert_mix,
    gate_weight,
    up_weight,
    down_weight,
):
    head_count = lax.axis_size("head")
    req_count = lax.axis_size("req")
    both = ("req", "head")
    requests, heads, width = queries.shape
    model = hidden.shape[1]
    quarter = model // head_count
    half = quarter // 2
    devices = req_count * head_count
    assert head_count == 4 and requests == ROWS - 1 and requests * EXPERTS <= quarter

    def swap(value, flip):
        return lax.ppermute(value, "head", [(n, n ^ flip) for n in range(head_count)])

    def on_hbm(*values):
        return [pltpu.with_memory_space_constraint(value, pltpu.HBM) for value in values]

    def fetch(after, *pieces):
        spans = tuple(span for _, span in pieces)
        shapes = tuple(pltpu.VMEM((last - first, model), bf16) for first, last in spans)
        size = sum(last - first for first, last in spans) * model * 2
        return pl.pallas_call(
            functools.partial(fetch_kernel, spans),
            out_shape=shapes,
            in_specs=[ANY] * (len(pieces) + 1),
            out_specs=[VMEM] * len(pieces),
            scratch_shapes=[pltpu.SemaphoreType.DMA((len(pieces),))],
            compiler_params=limit(4),
            cost_estimate=pl.CostEstimate(flops=0, bytes_accessed=size, transcendentals=0),
            name="fetch",
        )(*on_hbm(*(weight for weight, _ in pieces)), after)

    slots, _, depth = gate_weight.shape
    units = slots * depth
    chunk = units // 11
    split_a, split_b, split_c = 2 * chunk, 5 * chunk, 6 * chunk
    gate = jnp.swapaxes(gate_weight, 1, 2)
    up = jnp.swapaxes(up_weight, 1, 2)
    cache = jnp.swapaxes(latent_cache, 1, 2)
    pages_here = cache.shape[0]
    rows = ROWS * ROWS
    q_far = swap(queries, 2)
    cache_near = swap(cache, 1)
    large = (queries, cache, value_up, out_proj, hidden, norm_gain.reshape(1, model))
    usable, route, q_own, cache_own, value_up, out_proj, hidden, gain = pl.pallas_call(
        stage_kernel,
        out_shape=(
            pltpu.VMEM((2 * pages_here, rows, PAGE), f32),
            pltpu.VMEM((1, quarter), f32),
            *(pltpu.VMEM(value.shape, value.dtype) for value in large),
        ),
        in_specs=[ANY] * 10,
        out_specs=[VMEM] * 8,
        scratch_shapes=[
            pltpu.SMEM(page_table.shape[::-1], jnp.int32),
            pltpu.SMEM(seq_lens.shape, jnp.int32),
            pltpu.SMEM(expert_ids.shape, jnp.int32),
            pltpu.SMEM(expert_mix.shape, f32),
            pltpu.SemaphoreType.DMA((4,)),
            pltpu.SemaphoreType.DMA((6,)),
        ],
        compiler_params=limit(4),
        cost_estimate=pl.CostEstimate(flops=0, bytes_accessed=3 * 2**20, transcendentals=0),
        name="stage",
    )(*on_hbm(page_table.T, seq_lens, expert_ids, expert_mix, *large))
    own, own_lse, far = pl.pallas_call(
        attend_kernel,
        out_shape=(
            jax.ShapeDtypeStruct((heads, ROWS, RANK), f32),
            jax.ShapeDtypeStruct((heads, ROWS, LANES), f32),
            jax.ShapeDtypeStruct((heads, ROWS, RANK + LANES), bf16),
        ),
        in_specs=[VMEM] * 5,
        out_specs=[VMEM] * 3,
        scratch_shapes=[
            pltpu.VMEM((rows, width), f32),
            pltpu.VMEM((RANK // LANES, rows, LANES), f32),
            pltpu.VMEM((rows, LANES), f32),
        ],
        compiler_params=limit(8),
        name="attend",
    )(usable, q_own, q_far, cache_own, cache_near)
    gate_a, up_a = fetch(far, (gate, (0, split_a)), (up, (0, split_a)))
    far = swap(far, 2)
    piece = jax.ShapeDtypeStruct((ROWS, quarter), bf16)
    mine, near, far_y, far_both = pl.pallas_call(
        project_kernel,
        out_shape=(jax.ShapeDtypeStruct((ROWS, quarter), f32), piece, piece, piece),
        in_specs=[VMEM] * 6,
        out_specs=[VMEM] * 4,
        scratch_shapes=[pltpu.VMEM((ROWS, model), f32)],
        compiler_params=limit(8),
        name="project",
    )(own, own_lse, far, value_up, out_proj, gate_a)
    gate_b, up_b = fetch(near, (gate, (split_a, split_b)), (up, (split_a, split_b)))
    near, far_y, far_both = (
        lax.ppermute(piece, "head", [(n, (n + step) % head_count) for n in range(head_count)])
        for step, piece in ((1, near), (2, far_y), (3, far_both))
    )
    mixed, spread = pl.pallas_call(
        mix_kernel,
        out_shape=(
            jax.ShapeDtypeStruct((requests, quarter), f32),
            jax.ShapeDtypeStruct((devices, ROWS, half), bf16),
        ),
        in_specs=[VMEM] * 7,
        out_specs=[VMEM] * 2,
        compiler_params=limit(12),
        name="mix",
    )(mine, near, far_y, far_both, hidden, route, gate_b)
    tokens = lax.all_to_all(spread, both, split_axis=0, concat_axis=0, tiled=True)
    gate_c, up_c = fetch(tokens, (gate, (split_b, split_c)), (up, (split_b, split_c)))
    tokens_near = swap(tokens, 1)
    ready = (gate_a, up_a, gate_b, up_b, gate_c, up_c)
    theirs, active, down_own = pl.pallas_call(
        functools.partial(expert_kernel, chunk),
        out_shape=(
            jax.ShapeDtypeStruct((devices, ROWS, half), bf16),
            pltpu.VMEM((requests * req_count, units), bf16),
            pltpu.VMEM((units, model // 2), bf16),
        ),
        in_specs=[VMEM] * 9 + [ANY] * 3,
        out_specs=[VMEM] * 3,
        scratch_shapes=[
            pltpu.VMEM((model // LANES, ROWS * req_count, LANES), f32),
            pltpu.VMEM((requests * req_count, 3 * EXPERTS), f32),
            pltpu.VMEM((requests * req_count, units), bf16),
            pltpu.VMEM((model // 2 // LANES, ROWS * req_count, LANES), f32),
            pltpu.VMEM((units - split_c, model), bf16),
            pltpu.VMEM((units - split_c, model), bf16),
            pltpu.VMEM((units, model // 2), bf16),
            pltpu.SemaphoreType.DMA((2 + 2 * head_count,)),
        ],
        compiler_params=limit(32),
        name="experts",
    )(tokens, tokens_near, gain, *ready, *on_hbm(gate, up, down_weight))
    mine_half = pl.pallas_call(
        down_half,
        out_shape=jax.ShapeDtypeStruct((devices, ROWS, half), f32),
        in_specs=[VMEM] * 2,
        out_specs=VMEM,
        scratch_shapes=[pltpu.VMEM((model // 2 // LANES, ROWS * req_count, LANES), f32)],
        compiler_params=limit(12),
        cost_estimate=pl.CostEstimate(
            flops=2 * requests * req_count * units * model, bytes_accessed=units * model, transcendentals=0
        ),
        name="down",
    )(active, down_own)
    parts = pl.pallas_call(
        join_kernel,
        out_shape=jax.ShapeDtypeStruct((devices, ROWS, half), bf16),
        in_specs=[VMEM] * 2,
        out_specs=VMEM,
        compiler_params=limit(12),
        name="join",
    )(mine_half, swap(theirs, 1))
    parts = lax.all_to_all(parts, both, split_axis=0, concat_axis=0, tiled=True)
    return pl.pallas_call(
        final_kernel,
        out_shape=jax.ShapeDtypeStruct((requests, quarter), bf16),
        in_specs=[VMEM] * 2,
        out_specs=VMEM,
        compiler_params=limit(24),
        name="final",
    )(parts, mixed)


def solution(mesh):
    return jax.shard_map(
        per_device,
        mesh=mesh,
        in_specs=(
            P("req", None),
            P("req", "head", None),
            P(("req", "head"), None, None),
            P("req", None),
            P("req"),
            P("head", None, None),
            P("head", None),
            P(),
            P("req", None),
            P("req", None),
            P("req", None, "head"),
            P("req", None, "head"),
            P("req", "head", None),
        ),
        out_specs=P("req", "head"),
        check_vma=False,
    )
```

```python
import functools
import math

import jax
import jax.numpy as jnp
from jax import lax
from jax.experimental import pallas as pl
from jax.experimental.pallas import tpu as pltpu
from jax.sharding import PartitionSpec as P

RANK = 512
ROPE = 64
NOPE = 128
VHEAD = 128
EXPERTS = 64
TOP = 6
PAGE = 128
LANES = 128
ROWS = 8

norm_eps = 1e-06
masked_low = -1e30

f32 = jnp.float32
bf16 = jnp.bfloat16
NT = (((1,), (1,)), ((), ()))
VMEM = pl.BlockSpec(memory_space=pltpu.VMEM)
SMEM = pl.BlockSpec(memory_space=pltpu.SMEM)
ANY = pl.BlockSpec(memory_space=pl.ANY)


def split3(value):
    high = value.astype(bf16).astype(f32)
    rest = value - high
    middle = rest.astype(bf16).astype(f32)
    return high, middle, (rest - middle).astype(bf16).astype(f32)


def start_all(pairs, sems):
    copies = [
        pltpu.make_async_copy(src, dst, sems.at[n]) for n, (src, dst) in enumerate(pairs)
    ]
    for copy in copies:
        copy.start()
    return copies


def stage_kernel(*refs):
    table_in, lens_in, ids_in, mix_in = refs[:4]
    bias_out, route_out = refs[11:13]
    weight, first_out = refs[10], refs[19]
    table, lens, ids, mix, small_sems, sems = refs[20:]
    small = start_all(
        ((table_in, table), (lens_in, lens), (ids_in, ids), (mix_in, mix)), small_sems
    )
    flat = weight.reshape(weight.shape[0] * weight.shape[1], weight.shape[2])
    first = (flat.at[pl.ds(0, first_out.shape[0]), :], first_out)
    large = start_all((*zip(refs[4:10], refs[13:19]), first), sems)
    for copy in small:
        copy.wait()
    head_at = lax.axis_index("head")
    width, requests = table.shape
    pages_here = bias_out.shape[0] // 2
    row_request = lax.broadcasted_iota(jnp.int32, bias_out.shape[1:], 0) // ROWS
    within = lax.broadcasted_iota(jnp.int32, bias_out.shape[1:], 1)
    for side in range(2):
        for p in range(pages_here):
            page = (head_at ^ side) * pages_here + p
            owner = jnp.int32(-1)
            count = jnp.int32(0)
            for r in range(requests):
                for m in range(width):
                    left = lens[r] - m * PAGE
                    hit = jnp.logical_and(table[m, r] == page, left > 0)
                    owner = jnp.where(hit, r, owner)
                    count = jnp.where(hit, left, count)
            valid = (row_request == owner) & (within < count)
            bias_out[side * pages_here + p] = jnp.where(valid, 1.0, 0.0)
    lanes = lax.broadcasted_iota(jnp.int32, route_out.shape, 1)
    row = jnp.zeros(route_out.shape, f32)
    for r in range(requests):
        for i in range(TOP):
            row = jnp.where(lanes == r * EXPERTS + ids[r, i], mix[r, i], row)
    high, middle, low = split3(row)
    route_out[...] = jnp.where(
        head_at == 0, high, jnp.where(head_at == 1, middle, jnp.where(head_at == 2, low, 0.0))
    )
    for copy in large:
        copy.wait()


def fetch_kernel(spans, *refs):
    count = len(spans)
    sources, outs, sems = refs[:count], refs[count + 1 : 2 * count + 1], refs[2 * count + 1]
    pairs = []
    for source, out, (first, last) in zip(sources, outs, spans):
        flat = source.reshape(source.shape[0] * source.shape[1], source.shape[2])
        pairs.append((flat.at[pl.ds(first, last - first), :], out))
    for copy in start_all(tuple(pairs), sems):
        copy.wait()


def attend_kernel(
    usable,
    q_own,
    q_far,
    cache_own,
    cache_near,
    own_out,
    own_lse,
    far_out,
    q_all,
    weighted,
    lse_all,
):
    requests, heads, width = q_own.shape
    pages_here = cache_own.shape[0]
    q_all[requests * ROWS :, :] = jnp.zeros((ROWS * (ROWS - requests), width), f32)
    for r in range(requests):
        q_all[r * ROWS : r * ROWS + heads, :] = q_own[r].astype(f32)
        q_all[r * ROWS + heads : r * ROWS + 2 * heads, :] = q_far[r].astype(f32)
    q_rows = q_all[...].astype(bf16)
    total_rows = q_all.shape[0]
    scale = 1.0 / math.sqrt(NOPE + ROPE)
    keys = [cache.at[p] for cache in (cache_own, cache_near) for p in range(pages_here)]
    valids = [usable[n] > 0.0 for n in range(2 * pages_here)]
    scores = []
    for key, valid in zip(keys, valids):
        score = jnp.dot(q_rows, key[...], preferred_element_type=f32) * scale
        scores.append(jnp.where(valid, score, masked_low))
    highest = functools.reduce(jnp.maximum, scores).max(axis=-1, keepdims=True)
    total = jnp.zeros((total_rows, 1), f32)
    summed = jnp.zeros((total_rows, RANK), f32)
    for key, valid, score in zip(keys, valids, scores):
        weight = jnp.where(valid, jnp.exp(score - highest), 0.0)
        total = total + jnp.sum(weight, axis=-1, keepdims=True)
        high = weight.astype(bf16)
        low = (weight - high.astype(f32)).astype(bf16)
        latent = key[:RANK, :]
        summed = summed + lax.dot_general(high, latent, NT, preferred_element_type=f32)
        summed = summed + lax.dot_general(low, latent, NT, preferred_element_type=f32)
    some = total > 0.0
    safe = jnp.where(some, total, 1.0)
    summed = summed * (1.0 / safe)
    for c in range(RANK // LANES):
        weighted[c] = summed[:, c * LANES : (c + 1) * LANES]
    lse = jnp.where(some, highest + jnp.log(safe), masked_low)
    lse_all[...] = jnp.broadcast_to(lse, lse_all.shape)
    lane = lax.broadcasted_iota(jnp.int32, (ROWS, LANES), 1)
    for h in range(heads):
        own_lse[h] = lse_all[pl.ds(h, ROWS, stride=ROWS), :]
        for c in range(RANK // LANES):
            span = slice(c * LANES, (c + 1) * LANES)
            own_out[h, :, span] = weighted[c, pl.ds(h, ROWS, stride=ROWS), :]
            far_out[h, :, span] = weighted[c, pl.ds(heads + h, ROWS, stride=ROWS), :].astype(bf16)
        high, middle, low = split3(lse_all[pl.ds(heads + h, ROWS, stride=ROWS), :])
        far_out[h, :, RANK:] = jnp.where(
            lane == 0, high, jnp.where(lane == 1, middle, jnp.where(lane == 2, low, 0.0))
        ).astype(bf16)


def project_kernel(own, own_lse, far, value_up, out_proj, _, mine, near, far_y, far_both, whole):
    heads = own.shape[0]
    head_at = lax.axis_index("head")
    parts = []
    for h in range(heads):
        stats = far[h, :, RANK:].astype(f32)
        lse_far = stats[:, 0:1] + stats[:, 1:2] + stats[:, 2:3]
        lse_own = own_lse[h][:, 0:1]
        highest = jnp.maximum(lse_own, lse_far)
        weight_own = jnp.exp(lse_own - highest)
        weight_far = jnp.exp(lse_far - highest)
        merged = weight_own * own[h] + weight_far * far[h, :, :RANK].astype(f32)
        attended = (merged * (1.0 / (weight_own + weight_far))).astype(bf16)
        parts.append(jnp.dot(attended, value_up[h], preferred_element_type=f32))
    head_out = jnp.concatenate(parts, axis=1).astype(bf16)
    whole[...] = jnp.dot(head_out, out_proj[...], preferred_element_type=f32)
    quarter = mine.shape[1]
    mine[...] = whole[:, pl.ds(pl.multiple_of(head_at * quarter, quarter), quarter)]
    for out, flip in ((near, 1), (far_y, 2), (far_both, 3)):
        start = pl.multiple_of((head_at + flip) % 4 * quarter, quarter)
        out[...] = whole[:, pl.ds(start, quarter)].astype(bf16)


def mix_kernel(mine, near, far_y, far_both, hidden, route, _, mixed_out, spread_out):
    head_at = lax.axis_index("head")
    requests = hidden.shape[0]
    quarter = mine.shape[1]
    start = pl.multiple_of(head_at * quarter, quarter)
    attn = mine[...] + near[...].astype(f32) + far_y[...].astype(f32) + far_both[...].astype(f32)
    residual = hidden[:, pl.ds(start, quarter)].astype(f32)
    mixed_out[...] = attn[:requests] + residual
    row = lax.broadcasted_iota(jnp.int32, (ROWS, quarter), 0)
    padded = jnp.concatenate(
        [residual, jnp.zeros((ROWS - requests, quarter), f32)], axis=0
    )
    block = jnp.where(row < requests, attn + padded, route[...]).astype(bf16)
    half = spread_out.shape[2]
    for n in range(spread_out.shape[0]):
        spread_out[n] = block[:, n % 2 * half : (n % 2 + 1) * half]


def chunk_groups(first, last, chunk, count):
    chunks = (last - first) // chunk
    edges = [first + chunks * n // count * chunk for n in range(count + 1)]
    return list(zip(edges, edges[1:]))


def expert_kernel(
    chunk,
    tokens,
    tokens_near,
    gain,
    gate_z,
    gate_a,
    up_a,
    gate_b,
    up_b,
    gate_c,
    up_c,
    gate,
    up,
    down,
    theirs_out,
    active_out,
    down_own,
    rows_all,
    mix_all,
    active_all,
    total,
    gate_d,
    up_d,
    down_theirs,
    sems,
):
    req_count = lax.axis_size("req")
    head_count = lax.axis_size("head")
    req_at = lax.axis_index("req")
    slots, depth, model = down.shape
    quarter = model // head_count
    lower = lax.axis_index("head") % 2 == 0
    requests = ROWS - 1
    live = requests * req_count
    units = slots * depth
    ready = up_a.shape[0] + up_b.shape[0] + up_c.shape[0]
    pairs = []
    halves = chunk_groups(ready, units, chunk, 1)
    for first, last in halves:
        for source, buffer in ((gate, gate_d), (up, up_d)):
            flat = source.reshape(units, model)
            pairs.append(
                (flat.at[pl.ds(first, last - first), :], buffer.at[pl.ds(first - ready, last - first), :])
            )
    half = quarter // 2
    flat = down.reshape(units, model)
    for buffer, at in ((down_theirs, jnp.where(lower, 1, 0)), (down_own, jnp.where(lower, 0, 1))):
        for j in range(head_count):
            start = pl.multiple_of((2 * j + at) * half, half)
            pairs.append((flat.at[:, pl.ds(start, half)], buffer.at[:, pl.ds(j * half, half)]))
    loads = start_all(tuple(pairs), sems)
    for i in range(req_count):
        for j in range(head_count):
            here, there = (part[i * head_count + j].astype(f32) for part in (tokens, tokens_near))
            halves_of = (jnp.where(lower, here, there), jnp.where(lower, there, here))
            block = jnp.concatenate(halves_of, axis=1)
            for c in range(quarter // LANES):
                rows_all[j * quarter // LANES + c, pl.ds(i, ROWS, stride=req_count), :] = block[
                    :, c * LANES : (c + 1) * LANES
                ]
    for r in range(requests):
        for k in range(3):
            start = k * quarter + r * EXPERTS
            lane = start % LANES
            mix_all[r * req_count : (r + 1) * req_count, k * EXPERTS : (k + 1) * EXPERTS] = rows_all[
                start // LANES, live : live + req_count, lane : lane + EXPERTS
            ]
    mixed = jnp.concatenate([rows_all[c, :live, :] for c in range(model // LANES)], axis=1)
    spread = jnp.mean(mixed * mixed, axis=-1, keepdims=True)
    normed = (mixed * lax.rsqrt(spread + norm_eps) * gain[...]).astype(bf16)
    mix_rows = mix_all[...].astype(bf16)
    expert = lax.broadcasted_iota(jnp.int32, (max(slots, ROWS), 3 * EXPERTS), 1) % EXPERTS
    slot_at = req_at * slots + lax.broadcasted_iota(jnp.int32, expert.shape, 0)
    chosen = jnp.where(expert == slot_at // 2, 1.0, 0.0).astype(bf16)
    by_slot = lax.dot_general(chosen, mix_rows, NT, preferred_element_type=f32)
    gates, ups = (
        [(part, offset) for part in parts for offset in range(0, part.shape[0], chunk)]
        for parts in ((gate_z, gate_a, gate_b, gate_c, gate_d), (up_a, up_b, up_c, up_d))
    )
    for first, (gate_at, gate_from), (up_at, up_from) in zip(range(0, units, chunk), gates, ups):
        if first in [start for start, _ in halves]:
            loads.pop(0).wait()
            loads.pop(0).wait()
        unit = first + lax.broadcasted_iota(jnp.int32, (chunk, live), 0)
        weight = jnp.broadcast_to(by_slot[first // depth : first // depth + 1, :], (chunk, live))
        for slot in range(first // depth + 1, (first + chunk - 1) // depth + 1):
            weight = jnp.where(unit >= slot * depth, by_slot[slot : slot + 1, :], weight)
        gate_part = lax.dot_general(
            gate_at[gate_from : gate_from + chunk, :], normed, NT, preferred_element_type=f32
        )
        up_part = lax.dot_general(
            up_at[up_from : up_from + chunk, :], normed, NT, preferred_element_type=f32
        )
        active = gate_part / (1.0 + jnp.exp(-gate_part)) * up_part * weight
        active_all[:, first : first + chunk] = active.T.astype(bf16)
    for _ in range(head_count):
        loads.pop(0).wait()
    active_out[...] = active_all[...]
    down_half(active_all, down_theirs, theirs_out, total)
    for load in loads:
        load.wait()


def down_half(active, weights, out, total):
    groups, rows, _ = total.shape
    live = active.shape[0]
    req_count = rows // ROWS
    head_count = out.shape[0] // req_count
    product = jnp.dot(active[...], weights[...], preferred_element_type=f32)
    for c in range(groups):
        total[c, :live, :] = product[:, c * LANES : (c + 1) * LANES]
        total[c, live:, :] = jnp.zeros((req_count, LANES), f32)
    wide = groups // head_count
    for i in range(req_count):
        for j in range(head_count):
            for c in range(wide):
                out[i * head_count + j, :, c * LANES : (c + 1) * LANES] = total[
                    j * wide + c, pl.ds(i, ROWS, stride=req_count), :
                ].astype(out.dtype)


def join_kernel(mine, theirs, out):
    out[...] = (mine[...] + theirs[...].astype(f32)).astype(bf16)


def final_kernel(parts, mixed, out):
    halves = []
    for side in range(2):
        sources = [parts[n].astype(f32) for n in range(side, parts.shape[0], 2)]
        halves.append(functools.reduce(jnp.add, sources))
    total = jnp.concatenate(halves, axis=1)
    out[...] = (mixed[...] + total[: mixed.shape[0]]).astype(bf16)


def limit(mebibytes):
    return pltpu.CompilerParams(vmem_limit_bytes=mebibytes * 2**20)


def per_device(
    hidden,
    queries,
    latent_cache,
    page_table,
    seq_lens,
    value_up,
    out_proj,
    norm_gain,
    expert_ids,
    expert_mix,
    gate_weight,
    up_weight,
    down_weight,
):
    head_count = lax.axis_size("head")
    req_count = lax.axis_size("req")
    both = ("req", "head")
    requests, heads, width = queries.shape
    model = hidden.shape[1]
    quarter = model // head_count
    half = quarter // 2
    devices = req_count * head_count
    assert head_count == 4 and requests == ROWS - 1 and requests * EXPERTS <= quarter

    def swap(value, flip):
        return lax.ppermute(value, "head", [(n, n ^ flip) for n in range(head_count)])

    def on_hbm(*values):
        return [pltpu.with_memory_space_constraint(value, pltpu.HBM) for value in values]

    def fetch(after, *pieces):
        spans = tuple(span for _, span in pieces)
        shapes = tuple(pltpu.VMEM((last - first, model), bf16) for first, last in spans)
        size = sum(last - first for first, last in spans) * model * 2
        return pl.pallas_call(
            functools.partial(fetch_kernel, spans),
            out_shape=shapes,
            in_specs=[ANY] * (len(pieces) + 1),
            out_specs=[VMEM] * len(pieces),
            scratch_shapes=[pltpu.SemaphoreType.DMA((len(pieces),))],
            compiler_params=limit(4),
            cost_estimate=pl.CostEstimate(flops=0, bytes_accessed=size, transcendentals=0),
            name="fetch",
        )(*on_hbm(*(weight for weight, _ in pieces)), after)

    slots, _, depth = gate_weight.shape
    units = slots * depth
    chunk = units // 11
    split_z, up_a_end = chunk, 2 * chunk
    split_a, split_b, split_c = 3 * chunk, 5 * chunk, 6 * chunk
    gate = jnp.swapaxes(gate_weight, 1, 2)
    up = jnp.swapaxes(up_weight, 1, 2)
    cache = jnp.swapaxes(latent_cache, 1, 2)
    pages_here = cache.shape[0]
    rows = ROWS * ROWS
    q_far = swap(queries, 2)
    cache_near = swap(cache, 1)
    large = (queries, cache, value_up, out_proj, hidden, norm_gain.reshape(1, model))
    usable, route, q_own, cache_own, value_up, out_proj, hidden, gain, gate_z = pl.pallas_call(
        stage_kernel,
        out_shape=(
            pltpu.VMEM((2 * pages_here, rows, PAGE), f32),
            pltpu.VMEM((1, quarter), f32),
            *(pltpu.VMEM(value.shape, value.dtype) for value in large),
            pltpu.VMEM((split_z, model), bf16),
        ),
        in_specs=[ANY] * 11,
        out_specs=[VMEM] * 9,
        scratch_shapes=[
            pltpu.SMEM(page_table.shape[::-1], jnp.int32),
            pltpu.SMEM(seq_lens.shape, jnp.int32),
            pltpu.SMEM(expert_ids.shape, jnp.int32),
            pltpu.SMEM(expert_mix.shape, f32),
            pltpu.SemaphoreType.DMA((4,)),
            pltpu.SemaphoreType.DMA((7,)),
        ],
        compiler_params=limit(4),
        cost_estimate=pl.CostEstimate(flops=0, bytes_accessed=3 * 2**20, transcendentals=0),
        name="stage",
    )(*on_hbm(page_table.T, seq_lens, expert_ids, expert_mix, *large, gate))
    own, own_lse, far = pl.pallas_call(
        attend_kernel,
        out_shape=(
            jax.ShapeDtypeStruct((heads, ROWS, RANK), f32),
            jax.ShapeDtypeStruct((heads, ROWS, LANES), f32),
            jax.ShapeDtypeStruct((heads, ROWS, RANK + LANES), bf16),
        ),
        in_specs=[VMEM] * 5,
        out_specs=[VMEM] * 3,
        scratch_shapes=[
            pltpu.VMEM((rows, width), f32),
            pltpu.VMEM((RANK // LANES, rows, LANES), f32),
            pltpu.VMEM((rows, LANES), f32),
        ],
        compiler_params=limit(8),
        name="attend",
    )(usable, q_own, q_far, cache_own, cache_near)
    gate_a, up_a = fetch(far, (gate, (split_z, split_a)), (up, (0, up_a_end)))
    far = swap(far, 2)
    piece = jax.ShapeDtypeStruct((ROWS, quarter), bf16)
    mine, near, far_y, far_both = pl.pallas_call(
        project_kernel,
        out_shape=(jax.ShapeDtypeStruct((ROWS, quarter), f32), piece, piece, piece),
        in_specs=[VMEM] * 6,
        out_specs=[VMEM] * 4,
        scratch_shapes=[pltpu.VMEM((ROWS, model), f32)],
        compiler_params=limit(8),
        name="project",
    )(own, own_lse, far, value_up, out_proj, gate_a)
    gate_b, up_b = fetch(near, (gate, (split_a, split_b)), (up, (up_a_end, split_b)))
    near, far_y, far_both = (
        lax.ppermute(piece, "head", [(n, (n + step) % head_count) for n in range(head_count)])
        for step, piece in ((1, near), (2, far_y), (3, far_both))
    )
    mixed, spread = pl.pallas_call(
        mix_kernel,
        out_shape=(
            jax.ShapeDtypeStruct((requests, quarter), f32),
            jax.ShapeDtypeStruct((devices, ROWS, half), bf16),
        ),
        in_specs=[VMEM] * 7,
        out_specs=[VMEM] * 2,
        compiler_params=limit(12),
        name="mix",
    )(mine, near, far_y, far_both, hidden, route, gate_b)
    tokens = lax.all_to_all(spread, both, split_axis=0, concat_axis=0, tiled=True)
    gate_c, up_c = fetch(tokens, (gate, (split_b, split_c)), (up, (split_b, split_c)))
    tokens_near = swap(tokens, 1)
    ready = (gate_z, gate_a, up_a, gate_b, up_b, gate_c, up_c)
    theirs, active, down_own = pl.pallas_call(
        functools.partial(expert_kernel, chunk),
        out_shape=(
            jax.ShapeDtypeStruct((devices, ROWS, half), bf16),
            pltpu.VMEM((requests * req_count, units), bf16),
            pltpu.VMEM((units, model // 2), bf16),
        ),
        in_specs=[VMEM] * 10 + [ANY] * 3,
        out_specs=[VMEM] * 3,
        scratch_shapes=[
            pltpu.VMEM((model // LANES, ROWS * req_count, LANES), f32),
            pltpu.VMEM((requests * req_count, 3 * EXPERTS), f32),
            pltpu.VMEM((requests * req_count, units), bf16),
            pltpu.VMEM((model // 2 // LANES, ROWS * req_count, LANES), f32),
            pltpu.VMEM((units - split_c, model), bf16),
            pltpu.VMEM((units - split_c, model), bf16),
            pltpu.VMEM((units, model // 2), bf16),
            pltpu.SemaphoreType.DMA((2 + 2 * head_count,)),
        ],
        compiler_params=limit(32),
        name="experts",
    )(tokens, tokens_near, gain, *ready, *on_hbm(gate, up, down_weight))
    mine_half = pl.pallas_call(
        down_half,
        out_shape=jax.ShapeDtypeStruct((devices, ROWS, half), f32),
        in_specs=[VMEM] * 2,
        out_specs=VMEM,
        scratch_shapes=[pltpu.VMEM((model // 2 // LANES, ROWS * req_count, LANES), f32)],
        compiler_params=limit(12),
        cost_estimate=pl.CostEstimate(
            flops=2 * requests * req_count * units * model, bytes_accessed=units * model, transcendentals=0
        ),
        name="down",
    )(active, down_own)
    parts = pl.pallas_call(
        join_kernel,
        out_shape=jax.ShapeDtypeStruct((devices, ROWS, half), bf16),
        in_specs=[VMEM] * 2,
        out_specs=VMEM,
        compiler_params=limit(12),
        name="join",
    )(mine_half, swap(theirs, 1))
    parts = lax.all_to_all(parts, both, split_axis=0, concat_axis=0, tiled=True)
    return pl.pallas_call(
        final_kernel,
        out_shape=jax.ShapeDtypeStruct((requests, quarter), bf16),
        in_specs=[VMEM] * 2,
        out_specs=VMEM,
        compiler_params=limit(24),
        name="final",
    )(parts, mixed)


def solution(mesh):
    return jax.shard_map(
        per_device,
        mesh=mesh,
        in_specs=(
            P("req", None),
            P("req", "head", None),
            P(("req", "head"), None, None),
            P("req", None),
            P("req"),
            P("head", None, None),
            P("head", None),
            P(),
            P("req", None),
            P("req", None),
            P("req", None, "head"),
            P("req", None, "head"),
            P("req", "head", None),
        ),
        out_specs=P("req", "head"),
        check_vma=False,
    )
```

```python
import functools
import math

import jax
import jax.numpy as jnp
from jax import lax
from jax.experimental import pallas as pl
from jax.experimental.pallas import tpu as pltpu
from jax.sharding import PartitionSpec as P

RANK = 512
ROPE = 64
NOPE = 128
VHEAD = 128
EXPERTS = 64
TOP = 6
PAGE = 128
LANES = 128
ROWS = 8

norm_eps = 1e-06
masked_low = -1e30

f32 = jnp.float32
bf16 = jnp.bfloat16
NT = (((1,), (1,)), ((), ()))
VMEM = pl.BlockSpec(memory_space=pltpu.VMEM)
SMEM = pl.BlockSpec(memory_space=pltpu.SMEM)
ANY = pl.BlockSpec(memory_space=pl.ANY)


def split3(value):
    high = value.astype(bf16).astype(f32)
    rest = value - high
    middle = rest.astype(bf16).astype(f32)
    return high, middle, (rest - middle).astype(bf16).astype(f32)


def start_all(pairs, sems):
    copies = [
        pltpu.make_async_copy(src, dst, sems.at[n]) for n, (src, dst) in enumerate(pairs)
    ]
    for copy in copies:
        copy.start()
    return copies


def stage_kernel(*refs):
    table_in, lens_in, ids_in, mix_in = refs[:4]
    bias_out, route_out = refs[11:13]
    weight, first_out = refs[10], refs[19]
    table, lens, ids, mix, small_sems, sems = refs[20:]
    small = start_all(
        ((table_in, table), (lens_in, lens), (ids_in, ids), (mix_in, mix)), small_sems
    )
    flat = weight.reshape(weight.shape[0] * weight.shape[1], weight.shape[2])
    first = (flat.at[pl.ds(0, first_out.shape[0]), :], first_out)
    large = start_all((*zip(refs[4:10], refs[13:19]), first), sems)
    for copy in small:
        copy.wait()
    head_at = lax.axis_index("head")
    width, requests = table.shape
    pages_here = bias_out.shape[0] // 2
    row_request = lax.broadcasted_iota(jnp.int32, bias_out.shape[1:], 0) // ROWS
    within = lax.broadcasted_iota(jnp.int32, bias_out.shape[1:], 1)
    for side in range(2):
        for p in range(pages_here):
            page = (head_at ^ side) * pages_here + p
            owner = jnp.int32(-1)
            count = jnp.int32(0)
            for r in range(requests):
                for m in range(width):
                    left = lens[r] - m * PAGE
                    hit = jnp.logical_and(table[m, r] == page, left > 0)
                    owner = jnp.where(hit, r, owner)
                    count = jnp.where(hit, left, count)
            valid = (row_request == owner) & (within < count)
            bias_out[side * pages_here + p] = jnp.where(valid, 1.0, 0.0)
    lanes = lax.broadcasted_iota(jnp.int32, route_out.shape, 1)
    row = jnp.zeros(route_out.shape, f32)
    for r in range(requests):
        for i in range(TOP):
            row = jnp.where(lanes == r * EXPERTS + ids[r, i], mix[r, i], row)
    high, middle, low = split3(row)
    route_out[...] = jnp.where(
        head_at == 0, high, jnp.where(head_at == 1, middle, jnp.where(head_at == 2, low, 0.0))
    )
    for copy in large:
        copy.wait()


def fetch_kernel(spans, *refs):
    count = len(spans)
    sources, outs, sems = refs[:count], refs[count + 1 : 2 * count + 1], refs[2 * count + 1]
    pairs = []
    for source, out, (first, last) in zip(sources, outs, spans):
        flat = source.reshape(source.shape[0] * source.shape[1], source.shape[2])
        pairs.append((flat.at[pl.ds(first, last - first), :], out))
    for copy in start_all(tuple(pairs), sems):
        copy.wait()


def attend_kernel(
    usable,
    q_own,
    q_far,
    cache_own,
    cache_near,
    own_out,
    own_lse,
    far_out,
    q_all,
    weighted,
    lse_all,
):
    requests, heads, width = q_own.shape
    pages_here = cache_own.shape[0]
    q_all[requests * ROWS :, :] = jnp.zeros((ROWS * (ROWS - requests), width), f32)
    for r in range(requests):
        q_all[r * ROWS : r * ROWS + heads, :] = q_own[r].astype(f32)
        q_all[r * ROWS + heads : r * ROWS + 2 * heads, :] = q_far[r].astype(f32)
    q_rows = q_all[...].astype(bf16)
    total_rows = q_all.shape[0]
    scale = 1.0 / math.sqrt(NOPE + ROPE)
    keys = [cache.at[p] for cache in (cache_own, cache_near) for p in range(pages_here)]
    valids = [usable[n] > 0.0 for n in range(2 * pages_here)]
    scores = []
    for key, valid in zip(keys, valids):
        score = jnp.dot(q_rows, key[...], preferred_element_type=f32) * scale
        scores.append(jnp.where(valid, score, masked_low))
    highest = functools.reduce(jnp.maximum, scores).max(axis=-1, keepdims=True)
    total = jnp.zeros((total_rows, 1), f32)
    summed = jnp.zeros((total_rows, RANK), f32)
    for key, valid, score in zip(keys, valids, scores):
        weight = jnp.where(valid, jnp.exp(score - highest), 0.0)
        total = total + jnp.sum(weight, axis=-1, keepdims=True)
        high = weight.astype(bf16)
        low = (weight - high.astype(f32)).astype(bf16)
        latent = key[:RANK, :]
        summed = summed + lax.dot_general(high, latent, NT, preferred_element_type=f32)
        summed = summed + lax.dot_general(low, latent, NT, preferred_element_type=f32)
    some = total > 0.0
    safe = jnp.where(some, total, 1.0)
    summed = summed * (1.0 / safe)
    for c in range(RANK // LANES):
        weighted[c] = summed[:, c * LANES : (c + 1) * LANES]
    lse = jnp.where(some, highest + jnp.log(safe), masked_low)
    lse_all[...] = jnp.broadcast_to(lse, lse_all.shape)
    lane = lax.broadcasted_iota(jnp.int32, (ROWS, LANES), 1)
    for h in range(heads):
        own_lse[h] = lse_all[pl.ds(h, ROWS, stride=ROWS), :]
        for c in range(RANK // LANES):
            span = slice(c * LANES, (c + 1) * LANES)
            own_out[h, :, span] = weighted[c, pl.ds(h, ROWS, stride=ROWS), :]
            far_out[h, :, span] = weighted[c, pl.ds(heads + h, ROWS, stride=ROWS), :].astype(bf16)
        high, middle, low = split3(lse_all[pl.ds(heads + h, ROWS, stride=ROWS), :])
        far_out[h, :, RANK:] = jnp.where(
            lane == 0, high, jnp.where(lane == 1, middle, jnp.where(lane == 2, low, 0.0))
        ).astype(bf16)


def project_kernel(own, own_lse, far, value_up, out_proj, _, mine, near, far_y, far_both, whole):
    heads = own.shape[0]
    head_at = lax.axis_index("head")
    parts = []
    for h in range(heads):
        stats = far[h, :, RANK:].astype(f32)
        lse_far = stats[:, 0:1] + stats[:, 1:2] + stats[:, 2:3]
        lse_own = own_lse[h][:, 0:1]
        highest = jnp.maximum(lse_own, lse_far)
        weight_own = jnp.exp(lse_own - highest)
        weight_far = jnp.exp(lse_far - highest)
        merged = weight_own * own[h] + weight_far * far[h, :, :RANK].astype(f32)
        attended = (merged * (1.0 / (weight_own + weight_far))).astype(bf16)
        parts.append(jnp.dot(attended, value_up[h], preferred_element_type=f32))
    head_out = jnp.concatenate(parts, axis=1).astype(bf16)
    whole[...] = jnp.dot(head_out, out_proj[...], preferred_element_type=f32)
    quarter = mine.shape[1]
    mine[...] = whole[:, pl.ds(pl.multiple_of(head_at * quarter, quarter), quarter)]
    for out, flip in ((near, 1), (far_y, 2), (far_both, 3)):
        start = pl.multiple_of((head_at + flip) % 4 * quarter, quarter)
        out[...] = whole[:, pl.ds(start, quarter)].astype(bf16)


def mix_kernel(mine, near, far_y, far_both, hidden, route, _, mixed_out, spread_out):
    head_at = lax.axis_index("head")
    requests = hidden.shape[0]
    quarter = mine.shape[1]
    start = pl.multiple_of(head_at * quarter, quarter)
    attn = mine[...] + near[...].astype(f32) + far_y[...].astype(f32) + far_both[...].astype(f32)
    residual = hidden[:, pl.ds(start, quarter)].astype(f32)
    mixed_out[...] = attn[:requests] + residual
    row = lax.broadcasted_iota(jnp.int32, (ROWS, quarter), 0)
    padded = jnp.concatenate(
        [residual, jnp.zeros((ROWS - requests, quarter), f32)], axis=0
    )
    block = jnp.where(row < requests, attn + padded, route[...]).astype(bf16)
    half = spread_out.shape[2]
    for n in range(spread_out.shape[0]):
        side = n // lax.axis_size("req") % 2
        spread_out[n] = block[:, side * half : (side + 1) * half]


def chunk_groups(first, last, chunk, count):
    chunks = (last - first) // chunk
    edges = [first + chunks * n // count * chunk for n in range(count + 1)]
    return list(zip(edges, edges[1:]))


def expert_kernel(
    chunk,
    tokens,
    tokens_near,
    gain,
    gate_z,
    gate_a,
    up_a,
    gate_b,
    up_b,
    gate_c,
    up_c,
    gate,
    up,
    down,
    theirs_out,
    active_out,
    down_own,
    rows_all,
    mix_all,
    active_all,
    total,
    gate_d,
    up_d,
    down_theirs,
    sems,
):
    req_count = lax.axis_size("req")
    head_count = lax.axis_size("head")
    req_at = lax.axis_index("req")
    slots, depth, model = down.shape
    quarter = model // head_count
    lower = lax.axis_index("head") % 2 == 0
    requests = ROWS - 1
    live = requests * req_count
    units = slots * depth
    ready = up_a.shape[0] + up_b.shape[0] + up_c.shape[0]
    pairs = []
    halves = chunk_groups(ready, units, chunk, 1)
    for first, last in halves:
        for source, buffer in ((gate, gate_d), (up, up_d)):
            flat = source.reshape(units, model)
            pairs.append(
                (flat.at[pl.ds(first, last - first), :], buffer.at[pl.ds(first - ready, last - first), :])
            )
    half = quarter // 2
    flat = down.reshape(units, model)
    for buffer, at in ((down_theirs, jnp.where(lower, 1, 0)), (down_own, jnp.where(lower, 0, 1))):
        for j in range(head_count):
            start = pl.multiple_of((2 * j + at) * half, half)
            pairs.append((flat.at[:, pl.ds(start, half)], buffer.at[:, pl.ds(j * half, half)]))
    loads = start_all(tuple(pairs), sems)
    for i in range(req_count):
        for j in range(head_count):
            here, there = (part[j * req_count + i].astype(f32) for part in (tokens, tokens_near))
            halves_of = (jnp.where(lower, here, there), jnp.where(lower, there, here))
            block = jnp.concatenate(halves_of, axis=1)
            for c in range(quarter // LANES):
                rows_all[j * quarter // LANES + c, pl.ds(i, ROWS, stride=req_count), :] = block[
                    :, c * LANES : (c + 1) * LANES
                ]
    for r in range(requests):
        for k in range(3):
            start = k * quarter + r * EXPERTS
            lane = start % LANES
            mix_all[r * req_count : (r + 1) * req_count, k * EXPERTS : (k + 1) * EXPERTS] = rows_all[
                start // LANES, live : live + req_count, lane : lane + EXPERTS
            ]
    mixed = jnp.concatenate([rows_all[c, :live, :] for c in range(model // LANES)], axis=1)
    spread = jnp.mean(mixed * mixed, axis=-1, keepdims=True)
    normed = (mixed * lax.rsqrt(spread + norm_eps) * gain[...]).astype(bf16)
    mix_rows = mix_all[...].astype(bf16)
    expert = lax.broadcasted_iota(jnp.int32, (max(slots, ROWS), 3 * EXPERTS), 1) % EXPERTS
    slot_at = req_at * slots + lax.broadcasted_iota(jnp.int32, expert.shape, 0)
    chosen = jnp.where(expert == slot_at // 2, 1.0, 0.0).astype(bf16)
    by_slot = lax.dot_general(chosen, mix_rows, NT, preferred_element_type=f32)
    gates, ups = (
        [(part, offset) for part in parts for offset in range(0, part.shape[0], chunk)]
        for parts in ((gate_z, gate_a, gate_b, gate_c, gate_d), (up_a, up_b, up_c, up_d))
    )
    for first, (gate_at, gate_from), (up_at, up_from) in zip(range(0, units, chunk), gates, ups):
        if first in [start for start, _ in halves]:
            loads.pop(0).wait()
            loads.pop(0).wait()
        unit = first + lax.broadcasted_iota(jnp.int32, (chunk, live), 0)
        weight = jnp.broadcast_to(by_slot[first // depth : first // depth + 1, :], (chunk, live))
        for slot in range(first // depth + 1, (first + chunk - 1) // depth + 1):
            weight = jnp.where(unit >= slot * depth, by_slot[slot : slot + 1, :], weight)
        gate_part = lax.dot_general(
            gate_at[gate_from : gate_from + chunk, :], normed, NT, preferred_element_type=f32
        )
        up_part = lax.dot_general(
            up_at[up_from : up_from + chunk, :], normed, NT, preferred_element_type=f32
        )
        active = gate_part / (1.0 + jnp.exp(-gate_part)) * up_part * weight
        active_all[:, first : first + chunk] = active.T.astype(bf16)
    for _ in range(head_count):
        loads.pop(0).wait()
    active_out[...] = active_all[...]
    down_half(active_all, down_theirs, theirs_out, total)
    for load in loads:
        load.wait()


def down_half(active, weights, out, total):
    groups, rows, _ = total.shape
    live = active.shape[0]
    req_count = rows // ROWS
    head_count = out.shape[0] // req_count
    product = jnp.dot(active[...], weights[...], preferred_element_type=f32)
    for c in range(groups):
        total[c, :live, :] = product[:, c * LANES : (c + 1) * LANES]
        total[c, live:, :] = jnp.zeros((req_count, LANES), f32)
    wide = groups // head_count
    for i in range(req_count):
        for j in range(head_count):
            for c in range(wide):
                out[j * req_count + i, :, c * LANES : (c + 1) * LANES] = total[
                    j * wide + c, pl.ds(i, ROWS, stride=req_count), :
                ].astype(out.dtype)


def join_kernel(mine, theirs, out):
    out[...] = (mine[...] + theirs[...].astype(f32)).astype(bf16)


def final_kernel(parts, mixed, out):
    halves = []
    for side in range(2):
        places = [n for n in range(parts.shape[0]) if n // lax.axis_size("req") % 2 == side]
        sources = [parts[n].astype(f32) for n in places]
        halves.append(functools.reduce(jnp.add, sources))
    total = jnp.concatenate(halves, axis=1)
    out[...] = (mixed[...] + total[: mixed.shape[0]]).astype(bf16)


def limit(mebibytes):
    return pltpu.CompilerParams(vmem_limit_bytes=mebibytes * 2**20)


def per_device(
    hidden,
    queries,
    latent_cache,
    page_table,
    seq_lens,
    value_up,
    out_proj,
    norm_gain,
    expert_ids,
    expert_mix,
    gate_weight,
    up_weight,
    down_weight,
):
    head_count = lax.axis_size("head")
    req_count = lax.axis_size("req")
    both = ("head", "req")
    requests, heads, width = queries.shape
    model = hidden.shape[1]
    quarter = model // head_count
    half = quarter // 2
    devices = req_count * head_count
    assert head_count == 4 and requests == ROWS - 1 and requests * EXPERTS <= quarter

    def swap(value, flip):
        return lax.ppermute(value, "head", [(n, n ^ flip) for n in range(head_count)])

    def on_hbm(*values):
        return [pltpu.with_memory_space_constraint(value, pltpu.HBM) for value in values]

    def fetch(after, *pieces):
        spans = tuple(span for _, span in pieces)
        shapes = tuple(pltpu.VMEM((last - first, model), bf16) for first, last in spans)
        size = sum(last - first for first, last in spans) * model * 2
        return pl.pallas_call(
            functools.partial(fetch_kernel, spans),
            out_shape=shapes,
            in_specs=[ANY] * (len(pieces) + 1),
            out_specs=[VMEM] * len(pieces),
            scratch_shapes=[pltpu.SemaphoreType.DMA((len(pieces),))],
            compiler_params=limit(4),
            cost_estimate=pl.CostEstimate(flops=0, bytes_accessed=size, transcendentals=0),
            name="fetch",
        )(*on_hbm(*(weight for weight, _ in pieces)), after)

    slots, _, depth = gate_weight.shape
    units = slots * depth
    chunk = units // 11
    split_z, up_a_end = chunk, 2 * chunk
    split_a, split_b, split_c = 3 * chunk, 5 * chunk, 6 * chunk
    gate = jnp.swapaxes(gate_weight, 1, 2)
    up = jnp.swapaxes(up_weight, 1, 2)
    cache = jnp.swapaxes(latent_cache, 1, 2)
    pages_here = cache.shape[0]
    rows = ROWS * ROWS
    q_far = swap(queries, 2)
    cache_near = swap(cache, 1)
    large = (queries, cache, value_up, out_proj, hidden, norm_gain.reshape(1, model))
    usable, route, q_own, cache_own, value_up, out_proj, hidden, gain, gate_z = pl.pallas_call(
        stage_kernel,
        out_shape=(
            pltpu.VMEM((2 * pages_here, rows, PAGE), f32),
            pltpu.VMEM((1, quarter), f32),
            *(pltpu.VMEM(value.shape, value.dtype) for value in large),
            pltpu.VMEM((split_z, model), bf16),
        ),
        in_specs=[ANY] * 11,
        out_specs=[VMEM] * 9,
        scratch_shapes=[
            pltpu.SMEM(page_table.shape[::-1], jnp.int32),
            pltpu.SMEM(seq_lens.shape, jnp.int32),
            pltpu.SMEM(expert_ids.shape, jnp.int32),
            pltpu.SMEM(expert_mix.shape, f32),
            pltpu.SemaphoreType.DMA((4,)),
            pltpu.SemaphoreType.DMA((7,)),
        ],
        compiler_params=limit(4),
        cost_estimate=pl.CostEstimate(flops=0, bytes_accessed=3 * 2**20, transcendentals=0),
        name="stage",
    )(*on_hbm(page_table.T, seq_lens, expert_ids, expert_mix, *large, gate))
    own, own_lse, far = pl.pallas_call(
        attend_kernel,
        out_shape=(
            jax.ShapeDtypeStruct((heads, ROWS, RANK), f32),
            jax.ShapeDtypeStruct((heads, ROWS, LANES), f32),
            jax.ShapeDtypeStruct((heads, ROWS, RANK + LANES), bf16),
        ),
        in_specs=[VMEM] * 5,
        out_specs=[VMEM] * 3,
        scratch_shapes=[
            pltpu.VMEM((rows, width), f32),
            pltpu.VMEM((RANK // LANES, rows, LANES), f32),
            pltpu.VMEM((rows, LANES), f32),
        ],
        compiler_params=limit(8),
        name="attend",
    )(usable, q_own, q_far, cache_own, cache_near)
    gate_a, up_a = fetch(far, (gate, (split_z, split_a)), (up, (0, up_a_end)))
    far = swap(far, 2)
    piece = jax.ShapeDtypeStruct((ROWS, quarter), bf16)
    mine, near, far_y, far_both = pl.pallas_call(
        project_kernel,
        out_shape=(jax.ShapeDtypeStruct((ROWS, quarter), f32), piece, piece, piece),
        in_specs=[VMEM] * 6,
        out_specs=[VMEM] * 4,
        scratch_shapes=[pltpu.VMEM((ROWS, model), f32)],
        compiler_params=limit(8),
        name="project",
    )(own, own_lse, far, value_up, out_proj, gate_a)
    gate_b, up_b = fetch(near, (gate, (split_a, split_b)), (up, (up_a_end, split_b)))
    near, far_y, far_both = (
        lax.ppermute(piece, "head", [(n, (n + step) % head_count) for n in range(head_count)])
        for step, piece in ((1, near), (2, far_y), (3, far_both))
    )
    mixed, spread = pl.pallas_call(
        mix_kernel,
        out_shape=(
            jax.ShapeDtypeStruct((requests, quarter), f32),
            jax.ShapeDtypeStruct((devices, ROWS, half), bf16),
        ),
        in_specs=[VMEM] * 7,
        out_specs=[VMEM] * 2,
        compiler_params=limit(12),
        name="mix",
    )(mine, near, far_y, far_both, hidden, route, gate_b)
    tokens = lax.all_to_all(spread, both, split_axis=0, concat_axis=0, tiled=True)
    gate_c, up_c = fetch(tokens, (gate, (split_b, split_c)), (up, (split_b, split_c)))
    tokens_near = swap(tokens, 1)
    ready = (gate_z, gate_a, up_a, gate_b, up_b, gate_c, up_c)
    theirs, active, down_own = pl.pallas_call(
        functools.partial(expert_kernel, chunk),
        out_shape=(
            jax.ShapeDtypeStruct((devices, ROWS, half), bf16),
            pltpu.VMEM((requests * req_count, units), bf16),
            pltpu.VMEM((units, model // 2), bf16),
        ),
        in_specs=[VMEM] * 10 + [ANY] * 3,
        out_specs=[VMEM] * 3,
        scratch_shapes=[
            pltpu.VMEM((model // LANES, ROWS * req_count, LANES), f32),
            pltpu.VMEM((requests * req_count, 3 * EXPERTS), f32),
            pltpu.VMEM((requests * req_count, units), bf16),
            pltpu.VMEM((model // 2 // LANES, ROWS * req_count, LANES), f32),
            pltpu.VMEM((units - split_c, model), bf16),
            pltpu.VMEM((units - split_c, model), bf16),
            pltpu.VMEM((units, model // 2), bf16),
            pltpu.SemaphoreType.DMA((2 + 2 * head_count,)),
        ],
        compiler_params=limit(32),
        name="experts",
    )(tokens, tokens_near, gain, *ready, *on_hbm(gate, up, down_weight))
    mine_half = pl.pallas_call(
        down_half,
        out_shape=jax.ShapeDtypeStruct((devices, ROWS, half), f32),
        in_specs=[VMEM] * 2,
        out_specs=VMEM,
        scratch_shapes=[pltpu.VMEM((model // 2 // LANES, ROWS * req_count, LANES), f32)],
        compiler_params=limit(12),
        cost_estimate=pl.CostEstimate(
            flops=2 * requests * req_count * units * model, bytes_accessed=units * model, transcendentals=0
        ),
        name="down",
    )(active, down_own)
    parts = pl.pallas_call(
        join_kernel,
        out_shape=jax.ShapeDtypeStruct((devices, ROWS, half), bf16),
        in_specs=[VMEM] * 2,
        out_specs=VMEM,
        compiler_params=limit(12),
        name="join",
    )(mine_half, swap(theirs, 1))
    parts = lax.all_to_all(parts, both, split_axis=0, concat_axis=0, tiled=True)
    return pl.pallas_call(
        final_kernel,
        out_shape=jax.ShapeDtypeStruct((requests, quarter), bf16),
        in_specs=[VMEM] * 2,
        out_specs=VMEM,
        compiler_params=limit(24),
        name="final",
    )(parts, mixed)


def solution(mesh):
    return jax.shard_map(
        per_device,
        mesh=mesh,
        in_specs=(
            P("req", None),
            P("req", "head", None),
            P(("req", "head"), None, None),
            P("req", None),
            P("req"),
            P("head", None, None),
            P("head", None),
            P(),
            P("req", None),
            P("req", None),
            P("req", None, "head"),
            P("req", None, "head"),
            P("req", "head", None),
        ),
        out_specs=P("req", "head"),
        check_vma=False,
    )
```

```python
import functools
import math

import jax
import jax.numpy as jnp
from jax import lax
from jax.experimental import pallas as pl
from jax.experimental.pallas import tpu as pltpu
from jax.sharding import PartitionSpec as P

RANK = 512
ROPE = 64
NOPE = 128
VHEAD = 128
EXPERTS = 64
TOP = 6
PAGE = 128
LANES = 128
ROWS = 8

norm_eps = 1e-06
masked_low = -1e30

f32 = jnp.float32
bf16 = jnp.bfloat16
NT = (((1,), (1,)), ((), ()))
VMEM = pl.BlockSpec(memory_space=pltpu.VMEM)
SMEM = pl.BlockSpec(memory_space=pltpu.SMEM)
ANY = pl.BlockSpec(memory_space=pl.ANY)


def split3(value):
    high = value.astype(bf16).astype(f32)
    rest = value - high
    middle = rest.astype(bf16).astype(f32)
    return high, middle, (rest - middle).astype(bf16).astype(f32)


def start_all(pairs, sems):
    copies = [
        pltpu.make_async_copy(src, dst, sems.at[n]) for n, (src, dst) in enumerate(pairs)
    ]
    for copy in copies:
        copy.start()
    return copies


def stage_kernel(*refs):
    table_in, lens_in, ids_in, mix_in = refs[:4]
    bias_out, route_out = refs[11:13]
    weight, first_out = refs[10], refs[19]
    table, lens, ids, mix, small_sems, sems = refs[20:]
    small = start_all(
        ((table_in, table), (lens_in, lens), (ids_in, ids), (mix_in, mix)), small_sems
    )
    flat = weight.reshape(weight.shape[0] * weight.shape[1], weight.shape[2])
    first = (flat.at[pl.ds(0, first_out.shape[0]), :], first_out)
    large = start_all((*zip(refs[4:10], refs[13:19]), first), sems)
    for copy in small:
        copy.wait()
    head_at = lax.axis_index("head")
    width, requests = table.shape
    pages_here = bias_out.shape[0] // 2
    row_request = lax.broadcasted_iota(jnp.int32, bias_out.shape[1:], 0) // ROWS
    within = lax.broadcasted_iota(jnp.int32, bias_out.shape[1:], 1)
    for side in range(2):
        for p in range(pages_here):
            page = (head_at ^ side) * pages_here + p
            owner = jnp.int32(-1)
            count = jnp.int32(0)
            for r in range(requests):
                for m in range(width):
                    left = lens[r] - m * PAGE
                    hit = jnp.logical_and(table[m, r] == page, left > 0)
                    owner = jnp.where(hit, r, owner)
                    count = jnp.where(hit, left, count)
            valid = (row_request == owner) & (within < count)
            bias_out[side * pages_here + p] = jnp.where(valid, 1.0, 0.0)
    lanes = lax.broadcasted_iota(jnp.int32, route_out.shape, 1)
    row = jnp.zeros(route_out.shape, f32)
    for r in range(requests):
        for i in range(TOP):
            row = jnp.where(lanes == r * EXPERTS + ids[r, i], mix[r, i], row)
    high, middle, low = split3(row)
    route_out[...] = jnp.where(
        head_at == 0, high, jnp.where(head_at == 1, middle, jnp.where(head_at == 2, low, 0.0))
    )
    for copy in large:
        copy.wait()


def fetch_kernel(spans, *refs):
    count = len(spans)
    sources, outs, sems = refs[:count], refs[count + 1 : 2 * count + 1], refs[2 * count + 1]
    pairs = []
    for source, out, (first, last) in zip(sources, outs, spans):
        flat = source.reshape(source.shape[0] * source.shape[1], source.shape[2])
        pairs.append((flat.at[pl.ds(first, last - first), :], out))
    for copy in start_all(tuple(pairs), sems):
        copy.wait()


def attend_kernel(
    usable,
    q_own,
    q_far,
    cache_own,
    cache_near,
    own_out,
    own_lse,
    far_out,
    q_all,
    weighted,
    lse_all,
):
    requests, heads, width = q_own.shape
    pages_here = cache_own.shape[0]
    q_all[requests * ROWS :, :] = jnp.zeros((ROWS * (ROWS - requests), width), f32)
    for r in range(requests):
        q_all[r * ROWS : r * ROWS + heads, :] = q_own[r].astype(f32)
        q_all[r * ROWS + heads : r * ROWS + 2 * heads, :] = q_far[r].astype(f32)
    q_rows = q_all[...].astype(bf16)
    total_rows = q_all.shape[0]
    scale = 1.0 / math.sqrt(NOPE + ROPE)
    keys = [cache.at[p] for cache in (cache_own, cache_near) for p in range(pages_here)]
    valids = [usable[n] > 0.0 for n in range(2 * pages_here)]
    scores = []
    for key, valid in zip(keys, valids):
        score = jnp.dot(q_rows, key[...], preferred_element_type=f32) * scale
        scores.append(jnp.where(valid, score, masked_low))
    highest = functools.reduce(jnp.maximum, scores).max(axis=-1, keepdims=True)
    total = jnp.zeros((total_rows, 1), f32)
    summed = jnp.zeros((total_rows, RANK), f32)
    for key, valid, score in zip(keys, valids, scores):
        weight = jnp.where(valid, jnp.exp(score - highest), 0.0)
        total = total + jnp.sum(weight, axis=-1, keepdims=True)
        high = weight.astype(bf16)
        low = (weight - high.astype(f32)).astype(bf16)
        latent = key[:RANK, :]
        summed = summed + lax.dot_general(high, latent, NT, preferred_element_type=f32)
        summed = summed + lax.dot_general(low, latent, NT, preferred_element_type=f32)
    some = total > 0.0
    safe = jnp.where(some, total, 1.0)
    summed = summed * (1.0 / safe)
    for c in range(RANK // LANES):
        weighted[c] = summed[:, c * LANES : (c + 1) * LANES]
    lse = jnp.where(some, highest + jnp.log(safe), masked_low)
    lse_all[...] = jnp.broadcast_to(lse, lse_all.shape)
    lane = lax.broadcasted_iota(jnp.int32, (ROWS, LANES), 1)
    for h in range(heads):
        own_lse[h] = lse_all[pl.ds(h, ROWS, stride=ROWS), :]
        for c in range(RANK // LANES):
            span = slice(c * LANES, (c + 1) * LANES)
            own_out[h, :, span] = weighted[c, pl.ds(h, ROWS, stride=ROWS), :]
            far_out[h, :, span] = weighted[c, pl.ds(heads + h, ROWS, stride=ROWS), :].astype(bf16)
        high, middle, low = split3(lse_all[pl.ds(heads + h, ROWS, stride=ROWS), :])
        far_out[h, :, RANK:] = jnp.where(
            lane == 0, high, jnp.where(lane == 1, middle, jnp.where(lane == 2, low, 0.0))
        ).astype(bf16)


def project_kernel(own, own_lse, far, value_up, out_proj, _, mine, near, far_y, far_both, whole):
    heads = own.shape[0]
    head_at = lax.axis_index("head")
    parts = []
    for h in range(heads):
        stats = far[h, :, RANK:].astype(f32)
        lse_far = stats[:, 0:1] + stats[:, 1:2] + stats[:, 2:3]
        lse_own = own_lse[h][:, 0:1]
        highest = jnp.maximum(lse_own, lse_far)
        weight_own = jnp.exp(lse_own - highest)
        weight_far = jnp.exp(lse_far - highest)
        merged = weight_own * own[h] + weight_far * far[h, :, :RANK].astype(f32)
        attended = (merged * (1.0 / (weight_own + weight_far))).astype(bf16)
        parts.append(jnp.dot(attended, value_up[h], preferred_element_type=f32))
    head_out = jnp.concatenate(parts, axis=1).astype(bf16)
    whole[...] = jnp.dot(head_out, out_proj[...], preferred_element_type=f32)
    quarter = mine.shape[1]
    mine[...] = whole[:, pl.ds(pl.multiple_of(head_at * quarter, quarter), quarter)]
    for out, flip in ((near, 1), (far_y, 2), (far_both, 3)):
        start = pl.multiple_of((head_at + flip) % 4 * quarter, quarter)
        out[...] = whole[:, pl.ds(start, quarter)].astype(bf16)


def mix_kernel(mine, near, far_y, far_both, hidden, route, _, mixed_out, spread_out):
    head_at = lax.axis_index("head")
    requests = hidden.shape[0]
    quarter = mine.shape[1]
    start = pl.multiple_of(head_at * quarter, quarter)
    attn = mine[...] + near[...].astype(f32) + far_y[...].astype(f32) + far_both[...].astype(f32)
    residual = hidden[:, pl.ds(start, quarter)].astype(f32)
    mixed_out[...] = attn[:requests] + residual
    row = lax.broadcasted_iota(jnp.int32, (ROWS, quarter), 0)
    padded = jnp.concatenate(
        [residual, jnp.zeros((ROWS - requests, quarter), f32)], axis=0
    )
    block = jnp.where(row < requests, attn + padded, route[...]).astype(bf16)
    half = spread_out.shape[2]
    for n in range(spread_out.shape[0]):
        side = n // lax.axis_size("req") % 2
        spread_out[n] = block[:, side * half : (side + 1) * half]


def chunk_groups(first, last, chunk, count):
    chunks = (last - first) // chunk
    edges = [first + chunks * n // count * chunk for n in range(count + 1)]
    return list(zip(edges, edges[1:]))


def expert_kernel(
    chunk,
    tokens,
    tokens_near,
    gain,
    gate_z,
    gate_a,
    up_a,
    gate_b,
    up_b,
    gate_c,
    up_c,
    gate,
    up,
    down,
    theirs_out,
    active_out,
    down_own,
    rows_all,
    mix_all,
    active_all,
    total,
    gate_d,
    up_d,
    down_theirs,
    sems,
):
    req_count = lax.axis_size("req")
    head_count = lax.axis_size("head")
    req_at = lax.axis_index("req")
    slots, depth, model = down.shape
    quarter = model // head_count
    lower = lax.axis_index("head") % 2 == 0
    requests = ROWS - 1
    live = requests * req_count
    units = slots * depth
    ready = up_a.shape[0] + up_b.shape[0] + up_c.shape[0]
    pairs = []
    halves = chunk_groups(ready, units, chunk, 1)
    for first, last in halves:
        for source, buffer in ((gate, gate_d), (up, up_d)):
            flat = source.reshape(units, model)
            pairs.append(
                (flat.at[pl.ds(first, last - first), :], buffer.at[pl.ds(first - ready, last - first), :])
            )
    half = quarter // 2
    flat = down.reshape(units, model)
    for buffer, at in ((down_theirs, jnp.where(lower, 1, 0)), (down_own, jnp.where(lower, 0, 1))):
        for j in range(head_count):
            start = pl.multiple_of((2 * j + at) * half, half)
            pairs.append((flat.at[:, pl.ds(start, half)], buffer.at[:, pl.ds(j * half, half)]))
    loads = start_all(tuple(pairs), sems)
    for i in range(req_count):
        for j in range(head_count):
            here, there = (part[j * req_count + i].astype(f32) for part in (tokens, tokens_near))
            halves_of = (jnp.where(lower, here, there), jnp.where(lower, there, here))
            block = jnp.concatenate(halves_of, axis=1)
            for c in range(quarter // LANES):
                rows_all[j * quarter // LANES + c, pl.ds(i, ROWS, stride=req_count), :] = block[
                    :, c * LANES : (c + 1) * LANES
                ]
    for r in range(requests):
        for k in range(3):
            start = k * quarter + r * EXPERTS
            lane = start % LANES
            mix_all[r * req_count : (r + 1) * req_count, k * EXPERTS : (k + 1) * EXPERTS] = rows_all[
                start // LANES, live : live + req_count, lane : lane + EXPERTS
            ]
    mixed = jnp.concatenate([rows_all[c, :live, :] for c in range(model // LANES)], axis=1)
    spread = jnp.mean(mixed * mixed, axis=-1, keepdims=True)
    normed = (mixed * lax.rsqrt(spread + norm_eps) * gain[...]).astype(bf16)
    mix_rows = mix_all[...].astype(bf16)
    expert = lax.broadcasted_iota(jnp.int32, (max(slots, ROWS), 3 * EXPERTS), 1) % EXPERTS
    slot_at = req_at * slots + lax.broadcasted_iota(jnp.int32, expert.shape, 0)
    chosen = jnp.where(expert == slot_at // 2, 1.0, 0.0).astype(bf16)
    by_slot = lax.dot_general(chosen, mix_rows, NT, preferred_element_type=f32)
    gates, ups = (
        [(part, offset) for part in parts for offset in range(0, part.shape[0], chunk)]
        for parts in ((gate_z, gate_a, gate_b, gate_c, gate_d), (up_a, up_b, up_c, up_d))
    )
    for first, (gate_at, gate_from), (up_at, up_from) in zip(range(0, units, chunk), gates, ups):
        if first in [start for start, _ in halves]:
            loads.pop(0).wait()
            loads.pop(0).wait()
        unit = first + lax.broadcasted_iota(jnp.int32, (chunk, live), 0)
        weight = jnp.broadcast_to(by_slot[first // depth : first // depth + 1, :], (chunk, live))
        for slot in range(first // depth + 1, (first + chunk - 1) // depth + 1):
            weight = jnp.where(unit >= slot * depth, by_slot[slot : slot + 1, :], weight)
        gate_part = lax.dot_general(
            gate_at[gate_from : gate_from + chunk, :], normed, NT, preferred_element_type=f32
        )
        up_part = lax.dot_general(
            up_at[up_from : up_from + chunk, :], normed, NT, preferred_element_type=f32
        )
        active = gate_part / (1.0 + jnp.exp(-gate_part)) * up_part * weight
        active_all[:, first : first + chunk] = active.T.astype(bf16)
    for _ in range(head_count):
        loads.pop(0).wait()
    active_out[...] = active_all[...]
    down_half(active_all, down_theirs, theirs_out, total)
    for load in loads:
        load.wait()


def down_half(active, weights, out, total):
    groups, rows, _ = total.shape
    live = active.shape[0]
    req_count = rows // ROWS
    head_count = out.shape[0] // req_count
    product = jnp.dot(active[...], weights[...], preferred_element_type=f32)
    for c in range(groups):
        total[c, :live, :] = product[:, c * LANES : (c + 1) * LANES]
        total[c, live:, :] = jnp.zeros((req_count, LANES), f32)
    wide = groups // head_count
    for i in range(req_count):
        for j in range(head_count):
            for c in range(wide):
                out[j * req_count + i, :, c * LANES : (c + 1) * LANES] = total[
                    j * wide + c, pl.ds(i, ROWS, stride=req_count), :
                ].astype(out.dtype)


def join_kernel(mine, theirs, out):
    out[...] = (mine[...] + theirs[...].astype(f32)).astype(bf16)


def final_kernel(parts, mixed, out):
    halves = []
    for side in range(2):
        places = [n for n in range(parts.shape[0]) if n // lax.axis_size("req") % 2 == side]
        sources = [parts[n].astype(f32) for n in places]
        halves.append(functools.reduce(jnp.add, sources))
    total = jnp.concatenate(halves, axis=1)
    out[...] = (mixed[...] + total[: mixed.shape[0]]).astype(bf16)


def limit(mebibytes):
    return pltpu.CompilerParams(vmem_limit_bytes=mebibytes * 2**20)


def per_device(
    hidden,
    queries,
    latent_cache,
    page_table,
    seq_lens,
    value_up,
    out_proj,
    norm_gain,
    expert_ids,
    expert_mix,
    gate_weight,
    up_weight,
    down_weight,
):
    head_count = lax.axis_size("head")
    req_count = lax.axis_size("req")
    both = ("head", "req")
    requests, heads, width = queries.shape
    model = hidden.shape[1]
    quarter = model // head_count
    half = quarter // 2
    devices = req_count * head_count
    assert head_count == 4 and requests == ROWS - 1 and requests * EXPERTS <= quarter

    def swap(value, flip):
        return lax.ppermute(value, "head", [(n, n ^ flip) for n in range(head_count)])

    def on_hbm(*values):
        return [pltpu.with_memory_space_constraint(value, pltpu.HBM) for value in values]

    def fetch(after, *pieces):
        spans = tuple(span for _, span in pieces)
        shapes = tuple(pltpu.VMEM((last - first, model), bf16) for first, last in spans)
        size = sum(last - first for first, last in spans) * model * 2
        return pl.pallas_call(
            functools.partial(fetch_kernel, spans),
            out_shape=shapes,
            in_specs=[ANY] * (len(pieces) + 1),
            out_specs=[VMEM] * len(pieces),
            scratch_shapes=[pltpu.SemaphoreType.DMA((len(pieces),))],
            compiler_params=limit(4),
            cost_estimate=pl.CostEstimate(flops=0, bytes_accessed=size, transcendentals=0),
            name="fetch",
        )(*on_hbm(*(weight for weight, _ in pieces)), after)

    slots, _, depth = gate_weight.shape
    units = slots * depth
    chunk = units // 11
    split_z, up_a_end = chunk, 2 * chunk
    split_a, split_b, split_c = 3 * chunk, 5 * chunk, 7 * chunk
    gate = jnp.swapaxes(gate_weight, 1, 2)
    up = jnp.swapaxes(up_weight, 1, 2)
    cache = jnp.swapaxes(latent_cache, 1, 2)
    pages_here = cache.shape[0]
    rows = ROWS * ROWS
    q_far = swap(queries, 2)
    cache_near = swap(cache, 1)
    large = (queries, cache, value_up, out_proj, hidden, norm_gain.reshape(1, model))
    usable, route, q_own, cache_own, value_up, out_proj, hidden, gain, gate_z = pl.pallas_call(
        stage_kernel,
        out_shape=(
            pltpu.VMEM((2 * pages_here, rows, PAGE), f32),
            pltpu.VMEM((1, quarter), f32),
            *(pltpu.VMEM(value.shape, value.dtype) for value in large),
            pltpu.VMEM((split_z, model), bf16),
        ),
        in_specs=[ANY] * 11,
        out_specs=[VMEM] * 9,
        scratch_shapes=[
            pltpu.SMEM(page_table.shape[::-1], jnp.int32),
            pltpu.SMEM(seq_lens.shape, jnp.int32),
            pltpu.SMEM(expert_ids.shape, jnp.int32),
            pltpu.SMEM(expert_mix.shape, f32),
            pltpu.SemaphoreType.DMA((4,)),
            pltpu.SemaphoreType.DMA((7,)),
        ],
        compiler_params=limit(4),
        cost_estimate=pl.CostEstimate(flops=0, bytes_accessed=3 * 2**20, transcendentals=0),
        name="stage",
    )(*on_hbm(page_table.T, seq_lens, expert_ids, expert_mix, *large, gate))
    own, own_lse, far = pl.pallas_call(
        attend_kernel,
        out_shape=(
            jax.ShapeDtypeStruct((heads, ROWS, RANK), f32),
            jax.ShapeDtypeStruct((heads, ROWS, LANES), f32),
            jax.ShapeDtypeStruct((heads, ROWS, RANK + LANES), bf16),
        ),
        in_specs=[VMEM] * 5,
        out_specs=[VMEM] * 3,
        scratch_shapes=[
            pltpu.VMEM((rows, width), f32),
            pltpu.VMEM((RANK // LANES, rows, LANES), f32),
            pltpu.VMEM((rows, LANES), f32),
        ],
        compiler_params=limit(8),
        name="attend",
    )(usable, q_own, q_far, cache_own, cache_near)
    gate_a, up_a = fetch(far, (gate, (split_z, split_a)), (up, (0, up_a_end)))
    far = swap(far, 2)
    piece = jax.ShapeDtypeStruct((ROWS, quarter), bf16)
    mine, near, far_y, far_both = pl.pallas_call(
        project_kernel,
        out_shape=(jax.ShapeDtypeStruct((ROWS, quarter), f32), piece, piece, piece),
        in_specs=[VMEM] * 6,
        out_specs=[VMEM] * 4,
        scratch_shapes=[pltpu.VMEM((ROWS, model), f32)],
        compiler_params=limit(8),
        name="project",
    )(own, own_lse, far, value_up, out_proj, gate_a)
    gate_b, up_b = fetch(near, (gate, (split_a, split_b)), (up, (up_a_end, split_b)))
    near, far_y, far_both = (
        lax.ppermute(piece, "head", [(n, (n + step) % head_count) for n in range(head_count)])
        for step, piece in ((1, near), (2, far_y), (3, far_both))
    )
    mixed, spread = pl.pallas_call(
        mix_kernel,
        out_shape=(
            jax.ShapeDtypeStruct((requests, quarter), f32),
            jax.ShapeDtypeStruct((devices, ROWS, half), bf16),
        ),
        in_specs=[VMEM] * 7,
        out_specs=[VMEM] * 2,
        compiler_params=limit(12),
        name="mix",
    )(mine, near, far_y, far_both, hidden, route, gate_b)
    tokens = lax.all_to_all(spread, both, split_axis=0, concat_axis=0, tiled=True)
    gate_c, up_c = fetch(tokens, (gate, (split_b, split_c)), (up, (split_b, split_c)))
    tokens_near = swap(tokens, 1)
    ready = (gate_z, gate_a, up_a, gate_b, up_b, gate_c, up_c)
    theirs, active, down_own = pl.pallas_call(
        functools.partial(expert_kernel, chunk),
        out_shape=(
            jax.ShapeDtypeStruct((devices, ROWS, half), bf16),
            pltpu.VMEM((requests * req_count, units), bf16),
            pltpu.VMEM((units, model // 2), bf16),
        ),
        in_specs=[VMEM] * 10 + [ANY] * 3,
        out_specs=[VMEM] * 3,
        scratch_shapes=[
            pltpu.VMEM((model // LANES, ROWS * req_count, LANES), f32),
            pltpu.VMEM((requests * req_count, 3 * EXPERTS), f32),
            pltpu.VMEM((requests * req_count, units), bf16),
            pltpu.VMEM((model // 2 // LANES, ROWS * req_count, LANES), f32),
            pltpu.VMEM((units - split_c, model), bf16),
            pltpu.VMEM((units - split_c, model), bf16),
            pltpu.VMEM((units, model // 2), bf16),
            pltpu.SemaphoreType.DMA((2 + 2 * head_count,)),
        ],
        compiler_params=limit(32),
        name="experts",
    )(tokens, tokens_near, gain, *ready, *on_hbm(gate, up, down_weight))
    mine_half = pl.pallas_call(
        down_half,
        out_shape=jax.ShapeDtypeStruct((devices, ROWS, half), f32),
        in_specs=[VMEM] * 2,
        out_specs=VMEM,
        scratch_shapes=[pltpu.VMEM((model // 2 // LANES, ROWS * req_count, LANES), f32)],
        compiler_params=limit(12),
        cost_estimate=pl.CostEstimate(
            flops=2 * requests * req_count * units * model, bytes_accessed=units * model, transcendentals=0
        ),
        name="down",
    )(active, down_own)
    parts = pl.pallas_call(
        join_kernel,
        out_shape=jax.ShapeDtypeStruct((devices, ROWS, half), bf16),
        in_specs=[VMEM] * 2,
        out_specs=VMEM,
        compiler_params=limit(12),
        name="join",
    )(mine_half, swap(theirs, 1))
    parts = lax.all_to_all(parts, both, split_axis=0, concat_axis=0, tiled=True)
    return pl.pallas_call(
        final_kernel,
        out_shape=jax.ShapeDtypeStruct((requests, quarter), bf16),
        in_specs=[VMEM] * 2,
        out_specs=VMEM,
        compiler_params=limit(24),
        name="final",
    )(parts, mixed)


def solution(mesh):
    return jax.shard_map(
        per_device,
        mesh=mesh,
        in_specs=(
            P("req", None),
            P("req", "head", None),
            P(("req", "head"), None, None),
            P("req", None),
            P("req"),
            P("head", None, None),
            P("head", None),
            P(),
            P("req", None),
            P("req", None),
            P("req", None, "head"),
            P("req", None, "head"),
            P("req", "head", None),
        ),
        out_specs=P("req", "head"),
        check_vma=False,
    )
```
